32 devices in a mesh: ctx: 8 (over z, y), shard: 4 (over x, core).
Axes of the slice: x: 2, y: 2, z: 4, core: 2. Of those that a mesh axis runs over, the one named last changes fastest.
Arguments:
- hidden: bfloat16 [4, 2048, 768], P('shard', 'ctx'), may hold values from -6 to 6
- cotangent: bfloat16 [4, 2048, 768], P('shard', 'ctx'), may hold values from -6 to 6
- query_proj: bfloat16 [768, 768], P('shard'), may hold values from -0.0546875 to 0.0546875
- key_proj: bfloat16 [768, 768], P('shard'), may hold values from -0.21875 to 0.21875
- value_proj: bfloat16 [768, 768], P('shard'), may hold values from -0.21875 to 0.21875
- out_proj: bfloat16 [768, 768], P('shard'), may hold values from -0.875 to 0.875
- gate_proj: bfloat16 [768, 2048], P('shard'), may hold values from -0.21875 to 0.21875
- up_proj: bfloat16 [768, 2048], P('shard'), may hold values from -0.21875 to 0.21875
- down_proj: bfloat16 [2048, 768], P('shard'), may hold values from -0.125 to 0.125
- first_gain: bfloat16 [768], P('shard'), may hold values from 0.5 to 1.5
- second_gain: bfloat16 [768], P('shard'), may hold values from 0.5 to 1.5
- global_gain: bfloat16 [768], P('shard'), may hold values from 0.5 to 1.5
- local_bias: bfloat16 [32, 12], P('shard'), may hold values from -4 to 4
- side_bias: bfloat16 [32, 12], P('shard'), may hold values from -4 to 4
- segments: int32 [4, 2048], P('shard'), may hold values from 0 to 1, as said below
- local_buckets: int32 [1023], replicated, may hold values from 0 to 31
- global_buckets: int32 [255], replicated, may hold values from 0 to 31
Outputs:
- outputs: bfloat16 [4, 2048, 768], P('shard', 'ctx')
- grad_hidden: bfloat16 [4, 2048, 768], P('shard', 'ctx')
- grad_query: float32 [768, 768], P('shard')
- grad_key: float32 [768, 768], P('shard')
- grad_value: float32 [768, 768], P('shard')
- grad_out: float32 [768, 768], P('shard')
- grad_gate: float32 [768, 2048], P('shard')
- grad_up: float32 [768, 2048], P('shard')
- grad_down: float32 [2048, 768], P('shard')
- grad_first: float32 [768], P('shard')
- grad_second: float32 [768], P('shard')
- grad_global: float32 [768], P('shard')
- grad_local: float32 [32, 12], P('shard')
- grad_side: float32 [32, 12], P('shard')
The draws below stay inside these ranges and needn't reach their ends.
Inputs may be any that keep to these rules, and one draw needn't show every extreme that they name: `segments`: segment numbers start at 0 in every sequence, never fall, rise by at most one from token to token, and change only at multiples of 16 tokens: every document is a whole number of 16-token blocks. Every sequence holds exactly max(2, 2) documents.
All inputs are finite; a program needn't handle non-finite values.
Results may differ from the reference program's by a relative error of at most 0.018.
Values may be sent and summed in bfloat16 or wider, within the bound.
No kernel may reach another device: no remote copies, remote signals or barrier semaphores. Data moves between devices by JAX's collectives and lax.ppermute only.
A program may use at most 384 MiB of HBM per device.

```python
import jax
import jax.numpy as jnp
from jax import lax

D = 768
H = 12
HD = 64
FF = 2048
NB = 32
GB = 16
HALF = 512
BLOCK = 256
SEQ_LEN = 2048
NSEQ = 4
NG = 128


def draw_segments(key, part):
    blocks = SEQ_LEN // GB
    documents = max(blocks // 64, 2)
    seq_keys = jax.random.split(key, NSEQ)
    orders = jax.vmap(lambda single: jax.random.permutation(single, blocks - 1))(seq_keys) + 1
    chosen = orders[:, :documents - 1].astype(jnp.int32)
    block_iota = jnp.arange(blocks, dtype=jnp.int32)
    flags = jnp.any(chosen[:, :, None] == block_iota[None, None, :], axis=1).astype(jnp.int32)
    labels = jnp.cumsum(flags, axis=1).astype(jnp.int32)
    return jnp.repeat(labels, GB, axis=1)


def set_ends(array, rng, least, high):
    shape = array.shape
    spot = [jax.random.randint(jax.random.fold_in(rng, axis), (), 0, shape[axis]) for axis in range(len(shape))]
    array = array.at[tuple(spot)].set(least)
    longest = shape.index(max(shape))
    spot[longest] = (spot[longest] + 1) % shape[longest]
    return array.at[tuple(spot)].set(high)


def levels(key, shape, cuts, low, high):
    level = 1.0
    for axis_at, parts in cuts:
        steps = jax.random.uniform(jax.random.fold_in(jax.random.fold_in(key, 6), axis_at), (parts,), jnp.float32, low / len(cuts), high / len(cuts))
        level = level * jnp.repeat(jnp.exp(steps), shape[axis_at] // parts).reshape((-1,) + (1,) * (len(shape) - 1 - axis_at))
    return level


def centred(own_key, shape, width, limit, cuts=(), kind=jnp.bfloat16):
    values = width * jax.random.normal(own_key, shape, jnp.float32)
    if cuts:
        values = values * levels(own_key, shape, cuts, -0.22, 0.18)
    return jnp.clip(values, -limit, limit).astype(kind)


def setup_inputs(seed: int = 0) -> dict:
    key_list = jax.random.split(jax.random.key(seed), 18)
    return {
        "hidden": centred(key_list[0], (NSEQ, SEQ_LEN, D), 1.0, 6.0, ((0, 4), (1, 8))),
        "cotangent": centred(key_list[1], (NSEQ, SEQ_LEN, D), 1.0, 6.0, ((0, 4), (1, 8))),
        "query_proj": centred(key_list[2], (D, D), (D * 16) ** -0.5, 0.0546875, ((0, 4),)),
        "key_proj": centred(key_list[3], (D, D), D ** -0.5, 0.21875, ((0, 4),)),
        "value_proj": centred(key_list[4], (D, D), D ** -0.5, 0.21875, ((0, 4),)),
        "out_proj": centred(key_list[5], (D, D), (max(D // 16, 1)) ** -0.5, 0.875, ((0, 4),)),
        "gate_proj": centred(key_list[6], (D, FF), D ** -0.5, 0.21875, ((0, 4),)),
        "up_proj": centred(key_list[7], (D, FF), D ** -0.5, 0.21875, ((0, 4),)),
        "down_proj": centred(key_list[8], (FF, D), FF ** -0.5, 0.125, ((0, 4),)),
        "first_gain": jnp.clip(1.0 + 0.1 * jax.random.normal(key_list[9], (D,), jnp.float32), 0.5, 1.5).astype(jnp.bfloat16),
        "second_gain": jnp.clip(1.0 + 0.1 * jax.random.normal(key_list[10], (D,), jnp.float32), 0.5, 1.5).astype(jnp.bfloat16),
        "global_gain": jnp.clip(1.0 + 0.1 * jax.random.normal(key_list[11], (D,), jnp.float32), 0.5, 1.5).astype(jnp.bfloat16),
        "local_bias": centred(key_list[12], (NB, H), 1.0, 4.0, ((0, 4),)),
        "side_bias": centred(key_list[13], (NB, H), 1.0, 4.0, ((0, 4),)),
        "segments": draw_segments(jax.random.fold_in(key_list[17], 71), 0),
        "local_buckets": set_ends(jax.random.randint(key_list[15], (2 * HALF - 1,), 0, NB), jax.random.fold_in(key_list[15], 1), 0, NB - 1).astype(jnp.int32),
        "global_buckets": set_ends(jax.random.randint(key_list[16], (2 * NG - 1,), 0, NB), jax.random.fold_in(key_list[16], 1), 0, NB - 1).astype(jnp.int32),
    }


EPS = 1e-06
NEG = -1e+30
HIGHEST = lax.Precision.HIGHEST

@jax.custom_vjp
def low(v):
    return lax.optimization_barrier(v.astype(jnp.bfloat16)).astype(jnp.float32)

@jax.custom_vjp
def low_back(v):
    return v

def low_keep(v):
    return (low(v), None)

def low_pass(kept, grad):
    return (grad,)

def back_keep(v):
    return (v, None)

def back_low(kept, grad):
    return (low(grad),)
low.defvjp(low_keep, low_pass)
low_back.defvjp(back_keep, back_low)

def rms_norm(values, gain_row):
    return values * lax.rsqrt(lax.optimization_barrier(jnp.mean(values * values, axis=-1, keepdims=True)) + EPS) * gain_row

def project(values, weight):
    return jnp.einsum('...i,ij->...j', values, weight, precision=HIGHEST)

def attend_sequence(queries, keys, values, side_keys, side_values, labels, near_bias, side_table):
    window_len = BLOCK + 2 * HALF
    key_pad = jnp.pad(keys, ((HALF, HALF), (0, 0)))
    value_pad = jnp.pad(values, ((HALF, HALF), (0, 0)))
    label_pad = jnp.pad(labels, (HALF, HALF), constant_values=-1)
    label_side = labels[::GB]
    side_key_heads = side_keys.reshape(NG, H, HD)
    side_value_heads = side_values.reshape(NG, H, HD)
    row_iota = jnp.arange(BLOCK, dtype=jnp.int32)[:, None]
    col_iota = jnp.arange(window_len, dtype=jnp.int32)[None, :]
    in_window = jnp.abs(col_iota - HALF - row_iota) < HALF
    global_iota = jnp.arange(NG, dtype=jnp.int32)[None, :]

    def one_block(block_index):
        first_row = block_index * BLOCK
        query_heads = lax.dynamic_slice_in_dim(queries, first_row, BLOCK, 0).reshape(BLOCK, H, HD)
        key_heads = lax.dynamic_slice_in_dim(key_pad, first_row, window_len, 0).reshape(window_len, H, HD)
        value_heads = lax.dynamic_slice_in_dim(value_pad, first_row, window_len, 0).reshape(window_len, H, HD)
        label_query = lax.dynamic_slice_in_dim(labels, first_row, BLOCK, 0)
        label_window = lax.dynamic_slice_in_dim(label_pad, first_row, window_len, 0)
        near_mask = in_window & (label_window[None, :] == label_query[:, None])
        far_mask = label_side[None, :] == label_query[:, None]
        side_index = global_iota - (first_row + row_iota) // GB + NG - 1
        far_bias = jnp.transpose(jnp.take(side_table, side_index, axis=0), (2, 0, 1))
        near_scores = low_back(jnp.einsum('ihd,jhd->hij', query_heads, key_heads, precision=HIGHEST) + near_bias)
        near_scores = jnp.where(near_mask[None], near_scores, NEG)
        far_scores = low_back(jnp.einsum('ihd,jhd->hij', query_heads, side_key_heads, precision=HIGHEST) + far_bias)
        far_scores = jnp.where(far_mask[None], far_scores, NEG)
        peak = jnp.maximum(lax.optimization_barrier(jnp.max(near_scores, axis=-1)), lax.optimization_barrier(jnp.max(far_scores, axis=-1)))
        total = lax.optimization_barrier(jnp.sum(jnp.exp(near_scores - peak[..., None]), axis=-1)) + lax.optimization_barrier(jnp.sum(jnp.exp(far_scores - peak[..., None]), axis=-1))
        logsum = peak + jnp.log(total)
        near_probs = low(jnp.exp(near_scores - logsum[..., None]))
        far_probs = low(jnp.exp(far_scores - logsum[..., None]))
        mixed = jnp.einsum('hij,jhd->ihd', near_probs, value_heads, precision=HIGHEST)
        mixed = mixed + jnp.einsum('hij,jhd->ihd', far_probs, side_value_heads, precision=HIGHEST)
        return mixed.reshape(BLOCK, D)
    blocks = lax.map(jax.checkpoint(one_block), jnp.arange(SEQ_LEN // BLOCK, dtype=jnp.int32))
    return blocks.reshape(SEQ_LEN, D)

def layer_forward(inputs, query_proj, key_proj, value_proj, out_proj, gate_proj, up_proj, down_proj, first_gain, second_gain, global_gain, local_bias, side_bias, segments, local_buckets, global_buckets):
    normed = low(rms_norm(inputs, first_gain))
    queries = low_back(low(project(normed, query_proj)))
    keys = low_back(low(project(normed, key_proj)))
    values = low_back(low(project(normed, value_proj)))
    block_sums = lax.optimization_barrier(jnp.sum(normed.reshape(NSEQ, NG, GB, D), axis=2))
    side_rows = low(rms_norm(block_sums, global_gain))
    side_keys = low(project(side_rows, key_proj))
    side_values = low(project(side_rows, value_proj))
    near_table = jnp.take(local_bias, local_buckets, axis=0)
    side_table = jnp.take(side_bias, global_buckets, axis=0)
    row_iota = jnp.arange(BLOCK, dtype=jnp.int32)[:, None]
    col_iota = jnp.arange(BLOCK + 2 * HALF, dtype=jnp.int32)[None, :]
    near_index = jnp.clip(col_iota - row_iota - 1, 0, 2 * HALF - 2)
    near_bias = jnp.transpose(jnp.take(near_table, near_index, axis=0), (2, 0, 1))
    attended = lax.map(lambda pieces: attend_sequence(*pieces, near_bias, side_table), (queries, keys, values, side_keys, side_values, segments))
    attended = low_back(low(attended))
    middle = inputs + low_back(project(attended, out_proj))
    ffn_in = low(rms_norm(middle, second_gain))
    gate = low_back(project(ffn_in, gate_proj))
    up_part = low_back(project(ffn_in, up_proj))
    product = low_back(low(jax.nn.gelu(gate, approximate=True) * up_part))
    return middle + low_back(project(product, down_proj))

def reference(hidden, cotangent, query_proj, key_proj, value_proj, out_proj, gate_proj, up_proj, down_proj, first_gain, second_gain, global_gain, local_bias, side_bias, segments, local_buckets, global_buckets):
    floats = tuple((item.astype(jnp.float32) for item in (hidden, query_proj, key_proj, value_proj, out_proj, gate_proj, up_proj, down_proj, first_gain, second_gain, global_gain, local_bias, side_bias)))

    def forward(*values):
        return layer_forward(*values, segments, local_buckets, global_buckets)
    result, pullback = jax.vjp(forward, *floats)
    gradients = pullback(cotangent.astype(jnp.float32))
    return (result.astype(jnp.bfloat16), gradients[0].astype(jnp.bfloat16), gradients[1], gradients[2], gradients[3], gradients[4], gradients[5], gradients[6], gradients[7], gradients[8], gradients[9], gradients[10], gradients[11], gradients[12])
```

```python
import jax
import jax.numpy as jnp
from jax import lax
from jax.experimental import pallas as pl
from jax.experimental.pallas import tpu as pltpu
from jax.sharding import PartitionSpec as P

H = 12
HD = 64
NB = 32
GB = 16
HALF = 512
LANES = 128
PAIRS = H * HD // LANES

EPS = 1e-06
NEG = -1e30
HIGHEST = lax.Precision.HIGHEST
VMEM_LIMIT = 60 << 20


def shifted(value, axis, by):
    length = lax.axis_size(axis)
    pairs = [(i, i + by) for i in range(length) if 0 <= i + by < length]
    return lax.ppermute(value, axis, pairs)


def dot_nn(left, right):
    return lax.dot_general(
        left, right, (((1,), (0,)), ((), ())), preferred_element_type=jnp.float32
    )


def dot_nt(left, right):
    return lax.dot_general(
        left, right, (((1,), (1,)), ((), ())), preferred_element_type=jnp.float32
    )


def dot_tn(left, right):
    return lax.dot_general(
        left, right, (((0,), (0,)), ((), ())), preferred_element_type=jnp.float32
    )


def rms_scale(values):
    return lax.rsqrt(jnp.mean(values * values, axis=-1, keepdims=True) + EPS)


def norm_back(upstream, normed_val, row_scale, gain_row):
    scaled = upstream * gain_row
    return row_scale * (scaled - normed_val * jnp.mean(scaled * normed_val, axis=-1, keepdims=True))


def head_mask(head):
    lane = lax.broadcasted_iota(jnp.int32, (1, LANES), 1)
    own = (lane < HD) if head == 0 else (lane >= HD)
    return own.astype(jnp.float32)


def fill_offsets(base_ref, head, table_ref):
    width = table_ref.shape[1]
    base = jnp.broadcast_to(base_ref[0, head : head + 1, :], (8, width))
    base = pltpu.roll(base, 0, 1, stride=1, stride_axis=0)
    for group in range(LANES // 8):
        table_ref[group * 8 : group * 8 + 8, :] = (
            pltpu.roll(base, group * 8, 1) if group else base
        )


def score_rows(score_ref, table_ref, far_ref, head, half, step, near_len):
    row = pl.multiple_of(half * LANES + step * GB, GB)
    start = LANES if half == 0 else 0
    bias = table_ref[pl.ds(pl.multiple_of(step * GB, GB), GB), start : start + near_len]
    near = score_ref[pl.ds(row, GB), :near_len] + bias
    far = score_ref[pl.ds(row, GB), near_len:] + far_ref[
        0, head, pl.ds(half * (LANES // GB) + step, 1), :
    ]
    return row, near, far


def forward_kernel(
    q_ref, k_ref, v_ref, q_label_ref, k_label_ref, base_ref, far_ref,
    out_ref, log_ref,
    table_ref, score_ref, prob_ref, total_ref,
):
    rows = q_ref.shape[0]
    near_len = table_ref.shape[1] - LANES
    keys = jnp.concatenate([k_ref[...], k_label_ref[...]], axis=1)
    out = None
    logs = None
    for head in range(2):
        mask = head_mask(head)
        query = jnp.concatenate(
            [q_ref[...] * mask.astype(jnp.bfloat16), q_label_ref[...]], axis=1
        )
        score_ref[...] = dot_nt(query, keys)
        fill_offsets(base_ref, head, table_ref)
        for half in range(rows // LANES):

            def body(step, carry, half=half, head=head):
                row, near, far = score_rows(
                    score_ref, table_ref, far_ref, head, half, step, near_len
                )
                peak = jnp.maximum(
                    jnp.max(near, axis=1, keepdims=True), jnp.max(far, axis=1, keepdims=True)
                )
                near = jnp.exp(near - peak)
                far = jnp.exp(far - peak)
                total = jnp.sum(near, axis=1, keepdims=True) + jnp.sum(far, axis=1, keepdims=True)
                prob_ref[pl.ds(row, GB), :near_len] = near.astype(jnp.bfloat16)
                prob_ref[pl.ds(row, GB), near_len:] = far.astype(jnp.bfloat16)
                total_ref[0, pl.ds(row, GB), :] = jnp.broadcast_to(total, (GB, LANES))
                total_ref[1, pl.ds(row, GB), :] = jnp.broadcast_to(
                    peak + jnp.log(total), (GB, LANES)
                )
                return carry

            lax.fori_loop(0, LANES // GB, body, 0, unroll=2)
        mixed = dot_nn(prob_ref[...], v_ref[...]) / total_ref[0] * mask
        out = mixed if out is None else out + mixed
        part = total_ref[1] * mask
        logs = part if logs is None else logs + part
    out_ref[...] = out.astype(jnp.bfloat16)
    log_ref[0] = logs


def backward_kernel(
    q_ref, k_ref, v_ref, g_ref, o_ref, log_ref, q_label_ref, k_label_ref, base_ref, far_ref,
    dq_ref, dk_ref, dv_ref, diag_ref, dfar_ref,
    table_ref, score_ref, dprob_ref, prob_ref, delta_ref, fold_ref, col_ref, q_two, g_two,
):
    rows = q_ref.shape[0]
    near_len = table_ref.shape[1] - LANES
    keys = jnp.concatenate([k_ref[...], k_label_ref[...]], axis=1)
    weighted = g_ref[...].astype(jnp.float32) * o_ref[...].astype(jnp.float32)
    for head in range(2):
        mask = head_mask(head)
        mask_low = mask.astype(jnp.bfloat16)
        own_q = q_ref[...] * mask_low
        own_g = g_ref[...] * mask_low
        q_two[head * rows : (head + 1) * rows, :] = own_q
        g_two[head * rows : (head + 1) * rows, :] = own_g
        query = jnp.concatenate([own_q, q_label_ref[...]], axis=1)
        score_ref[...] = dot_nt(query, keys)
        dprob_ref[...] = dot_nt(own_g, v_ref[...])
        fill_offsets(base_ref, head, table_ref)
        col_ref[0] = jnp.broadcast_to(
            jnp.sum(weighted * mask, axis=1, keepdims=True), (rows, LANES)
        )
        col_ref[1] = jnp.broadcast_to(
            log_ref[0, :, head * HD : head * HD + 1], (rows, LANES)
        )
        for half in range(rows // LANES):

            def body(step, carry, half=half, head=head):
                row, near, far = score_rows(
                    score_ref, table_ref, far_ref, head, half, step, near_len
                )
                center = col_ref[0, pl.ds(row, GB), 0:1]
                logs = col_ref[1, pl.ds(row, GB), 0:1]
                to_row = pl.multiple_of(head * rows + row, GB)
                near = jnp.exp(near - logs)
                far = jnp.exp(far - logs)
                prob_ref[pl.ds(to_row, GB), :near_len] = near.astype(jnp.bfloat16)
                prob_ref[pl.ds(to_row, GB), near_len:] = far.astype(jnp.bfloat16)
                near = near * (dprob_ref[pl.ds(row, GB), :near_len] - center)
                far = far * (dprob_ref[pl.ds(row, GB), near_len:] - center)
                delta_ref[pl.ds(to_row, GB), :near_len] = near.astype(jnp.bfloat16)
                delta_ref[pl.ds(to_row, GB), near_len:] = far.astype(jnp.bfloat16)
                at = pl.ds(pl.multiple_of(step * GB, GB), GB)
                if half == 0:
                    fold_ref[at, :LANES] = jnp.zeros((GB, LANES), jnp.float32)
                    fold_ref[at, LANES:] = near
                else:
                    fold_ref[at, :near_len] += near
                dfar_ref[0, head, pl.ds(half * (LANES // GB) + step, 1), :] = jnp.sum(
                    far, axis=0, keepdims=True
                )
                return carry

            lax.fori_loop(0, LANES // GB, body, 0, unroll=2)
        diag = fold_ref[0:8, :]
        width = table_ref.shape[1]
        for group in range(1, LANES // 8):
            diag = diag + pltpu.roll(fold_ref[group * 8 : group * 8 + 8, :], width - group * 8, 1)
        diag_ref[0, head] = diag
    low = dot_nn(delta_ref[:rows, :], k_ref[...]) * head_mask(0)
    high = dot_nn(delta_ref[rows:, :], k_ref[...]) * head_mask(1)
    dq_ref[...] = (low + high).astype(jnp.bfloat16)
    dk_ref[...] = dot_tn(q_two[...], delta_ref[...]).T.astype(jnp.bfloat16)
    dv_ref[...] = dot_tn(g_two[...], prob_ref[...]).T.astype(jnp.bfloat16)


def attention_specs(rows, total, width, far_len):
    col = lambda p: (0, p)
    return dict(
        q=pl.BlockSpec((rows, LANES), col),
        k=pl.BlockSpec((total, LANES), col),
        q_label=pl.BlockSpec((rows, LANES), lambda p: (0, 0)),
        k_label=pl.BlockSpec((total, LANES), lambda p: (0, 0)),
        base=pl.BlockSpec((1, 2, width), lambda p: (p, 0, 0)),
        far=pl.BlockSpec((1, 2, rows // GB, far_len), lambda p: (p, 0, 0, 0)),
        log=pl.BlockSpec((1, rows, LANES), lambda p: (p, 0, 0)),
        diag=pl.BlockSpec((1, 2, 8, width), lambda p: (p, 0, 0, 0)),
    )


def attention_forward(q, k, v, q_label, k_label, base, far):
    rows, total, width, far_len = q.shape[0], k.shape[0], base.shape[2], far.shape[3]
    s = attention_specs(rows, total, width, far_len)
    return pl.pallas_call(
        forward_kernel,
        grid=(PAIRS,),
        in_specs=[s["q"], s["k"], s["k"], s["q_label"], s["k_label"], s["base"], s["far"]],
        out_specs=[s["q"], s["log"]],
        out_shape=[
            jax.ShapeDtypeStruct((rows, PAIRS * LANES), jnp.bfloat16),
            jax.ShapeDtypeStruct((PAIRS, rows, LANES), jnp.float32),
        ],
        scratch_shapes=[
            pltpu.VMEM((LANES, width), jnp.float32),
            pltpu.VMEM((rows, total), jnp.float32),
            pltpu.VMEM((rows, total), jnp.bfloat16),
            pltpu.VMEM((2, rows, LANES), jnp.float32),
        ],
        compiler_params=pltpu.CompilerParams(vmem_limit_bytes=VMEM_LIMIT),
        name="attention_forward",
    )(q, k, v, q_label, k_label, base, far)


def attention_backward(q, k, v, g, o, logs, q_label, k_label, base, far):
    rows, total, width, far_len = q.shape[0], k.shape[0], base.shape[2], far.shape[3]
    s = attention_specs(rows, total, width, far_len)
    return pl.pallas_call(
        backward_kernel,
        grid=(PAIRS,),
        in_specs=[
            s["q"], s["k"], s["k"], s["q"], s["q"], s["log"],
            s["q_label"], s["k_label"], s["base"], s["far"],
        ],
        out_specs=[s["q"], s["k"], s["k"], s["diag"], s["far"]],
        out_shape=[
            jax.ShapeDtypeStruct((rows, PAIRS * LANES), jnp.bfloat16),
            jax.ShapeDtypeStruct((total, PAIRS * LANES), jnp.bfloat16),
            jax.ShapeDtypeStruct((total, PAIRS * LANES), jnp.bfloat16),
            jax.ShapeDtypeStruct((PAIRS, 2, 8, width), jnp.float32),
            jax.ShapeDtypeStruct((PAIRS, 2, rows // GB, far_len), jnp.float32),
        ],
        scratch_shapes=[
            pltpu.VMEM((LANES, width), jnp.float32),
            pltpu.VMEM((rows, total), jnp.float32),
            pltpu.VMEM((rows, total), jnp.float32),
            pltpu.VMEM((2 * rows, total), jnp.bfloat16),
            pltpu.VMEM((2 * rows, total), jnp.bfloat16),
            pltpu.VMEM((LANES, width), jnp.float32),
            pltpu.VMEM((2, rows, LANES), jnp.float32),
            pltpu.VMEM((2 * rows, LANES), jnp.bfloat16),
            pltpu.VMEM((2 * rows, LANES), jnp.bfloat16),
        ],
        compiler_params=pltpu.CompilerParams(vmem_limit_bytes=VMEM_LIMIT),
        name="attention_backward",
    )(q, k, v, g, o, logs, q_label, k_label, base, far)


def on_device(
    hidden, cotangent, query_proj, key_proj, value_proj, out_proj, gate_proj, up_proj,
    down_proj, first_gain, second_gain, global_gain, local_bias, side_bias,
    segments, local_buckets, global_buckets,
):
    x_own = hidden[0]
    cot = cotangent[0]
    rows, width = x_own.shape
    cycle_size = lax.axis_size("ctx")
    cycle_index = lax.axis_index("ctx")
    first_row = cycle_index * rows
    far_len = rows * cycle_size // GB
    own_blocks = rows // GB
    reach = HALF // rows
    near_len = rows + 2 * HALF

    left = [shifted(x_own, "ctx", d) for d in range(reach, 0, -1)]
    right = [shifted(x_own, "ctx", -d) for d in range(1, reach + 1)]
    window = jnp.concatenate(left + [x_own] + right, axis=0)

    gather = lambda a: lax.all_gather(a, "shard", axis=0, tiled=True)
    w_query, w_key, w_value, w_out = map(gather, (query_proj, key_proj, value_proj, out_proj))
    w_gate, w_up, w_down = map(gather, (gate_proj, up_proj, down_proj))
    small = jnp.concatenate(
        [first_gain, second_gain, global_gain, local_bias.reshape(-1), side_bias.reshape(-1)]
    )
    small = gather(small[None])
    cut = first_gain.shape[0]
    gain_one = small[:, :cut].reshape(-1).astype(jnp.float32)
    gain_two = small[:, cut : 2 * cut].reshape(-1).astype(jnp.float32)
    gain_side = small[:, 2 * cut : 3 * cut].reshape(-1).astype(jnp.float32)
    tab = local_bias.size
    near_tab = small[:, 3 * cut : 3 * cut + tab].reshape(NB, H)
    side_tab = small[:, 3 * cut + tab :].reshape(NB, H)

    bucket_iota = jnp.arange(NB, dtype=jnp.int32)[None, :]
    onehot_near = (local_buckets[:, None] == bucket_iota).astype(jnp.bfloat16)
    near_row = lax.dot_general(
        near_tab, onehot_near, (((0,), (1,)), ((), ())), preferred_element_type=jnp.float32
    )
    table_width = near_len + LANES
    base = jnp.pad(
        near_row,
        ((0, 0), (LANES + 1, table_width - LANES - 1 - near_row.shape[1])),
        constant_values=NEG,
    ).reshape(PAIRS, 2, table_width)
    far_start = far_len - own_blocks - cycle_index * own_blocks
    bucket_slice = lax.dynamic_slice_in_dim(global_buckets, far_start, far_len + own_blocks - 1, 0)
    onehot_side = (bucket_slice[:, None] == bucket_iota).astype(jnp.bfloat16)
    side_row = lax.dot_general(
        side_tab, onehot_side, (((0,), (1,)), ((), ())), preferred_element_type=jnp.float32
    )
    far = jnp.stack(
        [side_row[:, own_blocks - 1 - r : own_blocks - 1 - r + far_len] for r in range(own_blocks)],
        axis=1,
    ).reshape(PAIRS, 2, own_blocks, far_len)
    labels = segments[0]
    label_iota = jnp.arange(LANES, dtype=jnp.int32)[None, :]
    label_query = lax.dynamic_slice_in_dim(labels, first_row, rows, 0)
    label_pad = jnp.pad(labels, (HALF, HALF), constant_values=-1)
    label_window = lax.dynamic_slice_in_dim(label_pad, first_row, near_len, 0)
    label_keys = jnp.concatenate([label_window, labels[::GB]])
    q_label = (label_query[:, None] == label_iota).astype(jnp.bfloat16)
    k_label = jnp.where(label_keys[:, None] == label_iota, 0.0, NEG).astype(jnp.bfloat16)

    wide = window.astype(jnp.float32)
    scale_wide = rms_scale(wide)
    normed_wide = ((wide * scale_wide) * gain_one).astype(jnp.bfloat16)
    inputs = x_own.astype(jnp.float32)
    scale_one = rms_scale(inputs)
    normed_one = inputs * scale_one
    normed = (normed_one * gain_one).astype(jnp.bfloat16)
    block_sums = jnp.sum(normed.astype(jnp.float32).reshape(own_blocks, GB, width), axis=1)
    scale_side = rms_scale(block_sums)
    normed_side = block_sums * scale_side
    side_rows = (normed_side * gain_side).astype(jnp.bfloat16)
    all_rows = lax.all_gather(side_rows, "ctx", axis=0, tiled=True)
    key_rows = jnp.concatenate([normed_wide, all_rows], axis=0)
    queries = dot_nn(normed, w_query).astype(jnp.bfloat16)
    keys = dot_nn(key_rows, w_key).astype(jnp.bfloat16)
    values = dot_nn(key_rows, w_value).astype(jnp.bfloat16)
    attended, logs = attention_forward(queries, keys, values, q_label, k_label, base, far)
    middle = inputs + dot_nn(attended, w_out)
    scale_two = rms_scale(middle)
    normed_two = middle * scale_two
    ffn_in = (normed_two * gain_two).astype(jnp.bfloat16)
    gate_pre = dot_nn(ffn_in, w_gate)
    up_pre = dot_nn(ffn_in, w_up)
    gelu_out, gelu_pull = jax.vjp(lambda v: jax.nn.gelu(v, approximate=True), gate_pre)
    product = (gelu_out * up_pre).astype(jnp.bfloat16)
    outputs = (middle + dot_nn(product, w_down)).astype(jnp.bfloat16)

    down_grad = dot_tn(product, cot)
    product_grad = dot_nt(cot, w_down)
    gate_delta = gelu_pull(product_grad * up_pre)[0].astype(jnp.bfloat16)
    up_delta = (product_grad * gelu_out).astype(jnp.bfloat16)
    gate_grad = dot_tn(ffn_in, gate_delta)
    up_grad = dot_tn(ffn_in, up_delta)
    ffn_back = dot_nt(gate_delta, w_gate) + dot_nt(up_delta, w_up)
    second_part = jnp.sum(ffn_back * normed_two, axis=0)
    middle_grad = cot.astype(jnp.float32) + norm_back(ffn_back, normed_two, scale_two, gain_two)
    mixed_grad = middle_grad.astype(jnp.bfloat16)
    out_grad = dot_tn(attended, mixed_grad)
    attended_grad = dot_nt(mixed_grad, w_out).astype(jnp.bfloat16)

    dq, dk, dv, diag, dfar = attention_backward(
        queries, keys, values, attended_grad, attended, logs, q_label, k_label, base, far
    )
    query_grad = dot_tn(normed, dq)
    key_grad = dot_tn(key_rows, dk)
    value_grad = dot_tn(key_rows, dv)
    key_back = dot_nt(dk, w_key) + dot_nt(dv, w_value)
    own_start = reach * rows
    normed_back = dot_nt(dq, w_query) + key_back[own_start : own_start + rows]
    back_low = key_back.astype(jnp.bfloat16)
    for distance in range(1, reach + 1):
        for direction in (1, -1):
            at = (reach - direction * distance) * rows
            normed_back = normed_back + shifted(
                back_low[at : at + rows], "ctx", -direction * distance
            ).astype(jnp.float32)
    side_blocks = back_low[near_len:].reshape(cycle_size, own_blocks, width)
    side_blocks = lax.all_to_all(side_blocks, "ctx", 0, 0, tiled=True)
    side_back = jnp.sum(side_blocks.astype(jnp.float32), axis=0)
    global_part = jnp.sum(side_back * normed_side, axis=0)
    sums_grad = norm_back(side_back, normed_side, scale_side, gain_side)
    normed_back = (
        normed_back.reshape(own_blocks, GB, width) + sums_grad[:, None, :]
    ).reshape(rows, width)
    first_part = jnp.sum(normed_back * normed_one, axis=0)
    hidden_grad = (
        middle_grad + norm_back(normed_back, normed_one, scale_one, gain_one)
    ).astype(jnp.bfloat16)

    diag = diag.reshape(H, 8, table_width)
    near_sum = diag[:, 0]
    for r in range(1, 8):
        near_sum = near_sum + jnp.roll(diag[:, r], -r, axis=1)
    near_sum = near_sum[:, LANES + 1 : LANES + 2 * HALF]
    local_part = lax.dot_general(
        onehot_near.astype(jnp.float32), near_sum, (((0,), (1,)), ((), ())), precision=HIGHEST
    )
    dfar = dfar.reshape(H, own_blocks, far_len)
    side_sum = sum(
        jnp.pad(dfar[:, r], ((0, 0), (own_blocks - 1 - r, r))) for r in range(own_blocks)
    )
    side_part = lax.dot_general(
        onehot_side.astype(jnp.float32), side_sum, (((0,), (1,)), ((), ())), precision=HIGHEST
    )

    scatter = lambda a: lax.psum_scatter(
        a.astype(jnp.bfloat16), "shard", scatter_dimension=0, tiled=True
    )
    big = [scatter(a) for a in (query_grad, key_grad, value_grad, out_grad, gate_grad, up_grad, down_grad)]
    big = [lax.psum(a, "ctx").astype(jnp.float32) for a in big]
    tiny = jnp.concatenate(
        [a.reshape(-1) for a in (first_part, second_part, global_part, local_part, side_part)]
    )
    tiny = lax.psum(tiny.reshape(-1, LANES), ("ctx", "shard")).reshape(-1)
    shard = lax.axis_index("shard")
    done, at = [], 0
    for a in (first_part, second_part, global_part, local_part, side_part):
        whole = tiny[at : at + a.size].reshape(a.shape)
        at += a.size
        part = a.shape[0] // lax.axis_size("shard")
        done.append(lax.dynamic_slice_in_dim(whole, shard * part, part, 0))
    return (outputs[None], hidden_grad[None], *big, *done)


def solution(mesh):
    tokens = P("shard", "ctx", None)
    weight = P("shard", None)
    gain = P("shard")
    return jax.shard_map(
        on_device,
        mesh=mesh,
        in_specs=(tokens, tokens) + (weight,) * 7 + (gain,) * 3 + (weight,) * 3 + (P(), P()),
        out_specs=(tokens, tokens) + (weight,) * 7 + (gain,) * 3 + (weight,) * 2,
        check_vma=False,
    )
```

```python
import jax
import jax.numpy as jnp
from jax import lax
from jax.experimental import pallas as pl
from jax.experimental.pallas import tpu as pltpu
from jax.sharding import PartitionSpec as P

H = 12
HD = 64
NB = 32
GB = 16
HALF = 512
LANES = 128
PAIRS = H * HD // LANES

EPS = 1e-06
NEG = -1e30
HIGHEST = lax.Precision.HIGHEST
VMEM_LIMIT = 60 << 20


CTX = ("z", "y")
SHARD = ("x", "c")


def shifted(value, axis, by):
    length = lax.axis_size(axis)
    pairs = [(i, i + by) for i in range(length) if 0 <= i + by < length]
    return lax.ppermute(value, axis, pairs)


def swapped(value, axis, bit=1):
    return lax.ppermute(value, axis, [(i, i ^ bit) for i in range(lax.axis_size(axis))])


def pick(value, index, dim=0):
    return lax.dynamic_index_in_dim(value, index, dim, keepdims=False)


def bit_of(axis, bit):
    return (lax.axis_index(axis) // bit) % 2


def halves(value):
    return value.reshape(2, value.shape[0] // 2, *value.shape[1:])


def in_order(own, other, upper):
    return jnp.where(
        upper == 1, jnp.concatenate([other, own], axis=0), jnp.concatenate([own, other], axis=0)
    )


def add_low(left, right):
    return (left.astype(jnp.float32) + right.astype(jnp.float32)).astype(jnp.bfloat16)


def bits(axis):
    return [1 << k for k in range(lax.axis_size(axis).bit_length() - 1)]


def scatter_over(value, axis, order):
    for bit in order:
        both, mine = halves(value), bit_of(axis, bit)
        value = add_low(pick(both, mine), swapped(pick(both, 1 - mine), axis, bit))
    return value


def gather_over(value, axis, order):
    for bit in order:
        value = in_order(value, swapped(value, axis, bit), bit_of(axis, bit))
    return value


def over_lines(value):
    order = bits("z")
    value = scatter_over(value, "z", order)
    value = gather_over(value, "z", order[::-1])
    return gather_over(value, "y", [1])


def core_sums(grads, rows):
    core = lax.axis_index("c")
    split = [a.astype(jnp.bfloat16).reshape(2, 2, r, a.shape[1]) for a, r in zip(grads, rows)]
    got = [swapped(pick(a, 1 - core, 1), "c") for a in split]
    return [add_low(pick(a, core, 1), b) for a, b in zip(split, got)]


def scatter_planes(both):
    x, y = lax.axis_index("x"), lax.axis_index("y")
    cut = both.shape[3] // 2
    first, second = both[..., :cut], both[..., cut:]
    got_first = swapped(pick(first, 1 - x, 0), "x")
    got_second = swapped(pick(second, 1 - y, 1), "y")
    first = add_low(pick(first, x, 0), got_first)
    second = add_low(pick(second, y, 1), got_second)
    got_first = swapped(pick(first, 1 - y, 0), "y")
    got_second = swapped(pick(second, 1 - x, 0), "x")
    first = add_low(pick(first, y, 0), got_first)
    second = add_low(pick(second, x, 0), got_second)
    return jnp.concatenate([first, second], axis=1)


def dot_nn(left, right):
    return lax.dot_general(
        left, right, (((1,), (0,)), ((), ())), preferred_element_type=jnp.float32
    )


def dot_nt(left, right):
    return lax.dot_general(
        left, right, (((1,), (1,)), ((), ())), preferred_element_type=jnp.float32
    )


def dot_tn(left, right):
    return lax.dot_general(
        left, right, (((0,), (0,)), ((), ())), preferred_element_type=jnp.float32
    )


def rms_scale(values):
    return lax.rsqrt(jnp.mean(values * values, axis=-1, keepdims=True) + EPS)


def norm_back(upstream, normed_val, row_scale, gain_row):
    scaled = upstream * gain_row
    return row_scale * (scaled - normed_val * jnp.mean(scaled * normed_val, axis=-1, keepdims=True))


def head_mask(head):
    lane = lax.broadcasted_iota(jnp.int32, (1, LANES), 1)
    own = (lane < HD) if head == 0 else (lane >= HD)
    return own.astype(jnp.float32)


def fill_offsets(base_ref, head, table_ref):
    width = table_ref.shape[1]
    base = jnp.broadcast_to(base_ref[0, head : head + 1, :], (8, width))
    base = pltpu.roll(base, 0, 1, stride=1, stride_axis=0)
    for group in range(LANES // 8):
        table_ref[group * 8 : group * 8 + 8, :] = (
            pltpu.roll(base, group * 8, 1) if group else base
        )


def score_rows(score_ref, table_ref, far_ref, head, half, step, near_len):
    row = pl.multiple_of(half * LANES + step * GB, GB)
    start = LANES if half == 0 else 0
    bias = table_ref[pl.ds(pl.multiple_of(step * GB, GB), GB), start : start + near_len]
    near = score_ref[pl.ds(row, GB), :near_len] + bias
    far = score_ref[pl.ds(row, GB), near_len:] + far_ref[
        0, head, pl.ds(half * (LANES // GB) + step, 1), :
    ]
    return row, near, far


def forward_kernel(
    q_ref, k_ref, v_ref, q_label_ref, k_label_ref, base_ref, far_ref,
    out_ref, log_ref,
    table_ref, score_ref, prob_ref, total_ref,
):
    rows = q_ref.shape[0]
    near_len = table_ref.shape[1] - LANES
    keys = jnp.concatenate([k_ref[...], k_label_ref[...]], axis=1)
    out = None
    logs = None
    for head in range(2):
        mask = head_mask(head)
        query = jnp.concatenate(
            [q_ref[...] * mask.astype(jnp.bfloat16), q_label_ref[...]], axis=1
        )
        score_ref[...] = dot_nt(query, keys)
        fill_offsets(base_ref, head, table_ref)
        for half in range(rows // LANES):

            def body(step, carry, half=half, head=head):
                row, near, far = score_rows(
                    score_ref, table_ref, far_ref, head, half, step, near_len
                )
                peak = jnp.maximum(
                    jnp.max(near, axis=1, keepdims=True), jnp.max(far, axis=1, keepdims=True)
                )
                near = jnp.exp(near - peak)
                far = jnp.exp(far - peak)
                total = jnp.sum(near, axis=1, keepdims=True) + jnp.sum(far, axis=1, keepdims=True)
                prob_ref[pl.ds(row, GB), :near_len] = near.astype(jnp.bfloat16)
                prob_ref[pl.ds(row, GB), near_len:] = far.astype(jnp.bfloat16)
                total_ref[0, pl.ds(row, GB), :] = jnp.broadcast_to(total, (GB, LANES))
                total_ref[1, pl.ds(row, GB), :] = jnp.broadcast_to(
                    peak + jnp.log(total), (GB, LANES)
                )
                return carry

            lax.fori_loop(0, LANES // GB, body, 0, unroll=2)
        mixed = dot_nn(prob_ref[...], v_ref[...]) / total_ref[0] * mask
        out = mixed if out is None else out + mixed
        part = total_ref[1] * mask
        logs = part if logs is None else logs + part
    out_ref[...] = out.astype(jnp.bfloat16)
    log_ref[0] = logs


def backward_kernel(
    q_ref, k_ref, v_ref, g_ref, o_ref, log_ref, q_label_ref, k_label_ref, base_ref, far_ref,
    dq_ref, dk_ref, dv_ref, diag_ref, dfar_ref,
    table_ref, score_ref, dprob_ref, prob_ref, delta_ref, fold_ref, col_ref, q_two, g_two,
):
    rows = q_ref.shape[0]
    near_len = table_ref.shape[1] - LANES
    keys = jnp.concatenate([k_ref[...], k_label_ref[...]], axis=1)
    weighted = g_ref[...].astype(jnp.float32) * o_ref[...].astype(jnp.float32)
    for head in range(2):
        mask = head_mask(head)
        mask_low = mask.astype(jnp.bfloat16)
        own_q = q_ref[...] * mask_low
        own_g = g_ref[...] * mask_low
        q_two[head * rows : (head + 1) * rows, :] = own_q
        g_two[head * rows : (head + 1) * rows, :] = own_g
        query = jnp.concatenate([own_q, q_label_ref[...]], axis=1)
        score_ref[...] = dot_nt(query, keys)
        dprob_ref[...] = dot_nt(own_g, v_ref[...])
        fill_offsets(base_ref, head, table_ref)
        col_ref[0] = jnp.broadcast_to(
            jnp.sum(weighted * mask, axis=1, keepdims=True), (rows, LANES)
        )
        col_ref[1] = jnp.broadcast_to(
            log_ref[0, :, head * HD : head * HD + 1], (rows, LANES)
        )
        for half in range(rows // LANES):

            def body(step, carry, half=half, head=head):
                row, near, far = score_rows(
                    score_ref, table_ref, far_ref, head, half, step, near_len
                )
                center = col_ref[0, pl.ds(row, GB), 0:1]
                logs = col_ref[1, pl.ds(row, GB), 0:1]
                to_row = pl.multiple_of(head * rows + row, GB)
                near = jnp.exp(near - logs)
                far = jnp.exp(far - logs)
                prob_ref[pl.ds(to_row, GB), :near_len] = near.astype(jnp.bfloat16)
                prob_ref[pl.ds(to_row, GB), near_len:] = far.astype(jnp.bfloat16)
                near = near * (dprob_ref[pl.ds(row, GB), :near_len] - center)
                far = far * (dprob_ref[pl.ds(row, GB), near_len:] - center)
                delta_ref[pl.ds(to_row, GB), :near_len] = near.astype(jnp.bfloat16)
                delta_ref[pl.ds(to_row, GB), near_len:] = far.astype(jnp.bfloat16)
                at = pl.ds(pl.multiple_of(step * GB, GB), GB)
                if half == 0:
                    fold_ref[at, :LANES] = jnp.zeros((GB, LANES), jnp.float32)
                    fold_ref[at, LANES:] = near
                else:
                    fold_ref[at, :near_len] += near
                dfar_ref[0, head, pl.ds(half * (LANES // GB) + step, 1), :] = jnp.sum(
                    far, axis=0, keepdims=True
                )
                return carry

            lax.fori_loop(0, LANES // GB, body, 0, unroll=2)
        diag = fold_ref[0:8, :]
        width = table_ref.shape[1]
        for group in range(1, LANES // 8):
            diag = diag + pltpu.roll(fold_ref[group * 8 : group * 8 + 8, :], width - group * 8, 1)
        diag_ref[0, head] = diag
    low = dot_nn(delta_ref[:rows, :], k_ref[...]) * head_mask(0)
    high = dot_nn(delta_ref[rows:, :], k_ref[...]) * head_mask(1)
    dq_ref[...] = (low + high).astype(jnp.bfloat16)
    dk_ref[...] = dot_tn(q_two[...], delta_ref[...]).T.astype(jnp.bfloat16)
    dv_ref[...] = dot_tn(g_two[...], prob_ref[...]).T.astype(jnp.bfloat16)


def attention_specs(rows, total, width, far_len):
    col = lambda p: (0, p)
    return dict(
        q=pl.BlockSpec((rows, LANES), col),
        k=pl.BlockSpec((total, LANES), col),
        q_label=pl.BlockSpec((rows, LANES), lambda p: (0, 0)),
        k_label=pl.BlockSpec((total, LANES), lambda p: (0, 0)),
        base=pl.BlockSpec((1, 2, width), lambda p: (p, 0, 0)),
        far=pl.BlockSpec((1, 2, rows // GB, far_len), lambda p: (p, 0, 0, 0)),
        log=pl.BlockSpec((1, rows, LANES), lambda p: (p, 0, 0)),
        diag=pl.BlockSpec((1, 2, 8, width), lambda p: (p, 0, 0, 0)),
    )


def attention_forward(q, k, v, q_label, k_label, base, far):
    rows, total, width, far_len = q.shape[0], k.shape[0], base.shape[2], far.shape[3]
    s = attention_specs(rows, total, width, far_len)
    return pl.pallas_call(
        forward_kernel,
        grid=(PAIRS,),
        in_specs=[s["q"], s["k"], s["k"], s["q_label"], s["k_label"], s["base"], s["far"]],
        out_specs=[s["q"], s["log"]],
        out_shape=[
            jax.ShapeDtypeStruct((rows, PAIRS * LANES), jnp.bfloat16),
            jax.ShapeDtypeStruct((PAIRS, rows, LANES), jnp.float32),
        ],
        scratch_shapes=[
            pltpu.VMEM((LANES, width), jnp.float32),
            pltpu.VMEM((rows, total), jnp.float32),
            pltpu.VMEM((rows, total), jnp.bfloat16),
            pltpu.VMEM((2, rows, LANES), jnp.float32),
        ],
        compiler_params=pltpu.CompilerParams(vmem_limit_bytes=VMEM_LIMIT),
        name="attention_forward",
    )(q, k, v, q_label, k_label, base, far)


def attention_backward(q, k, v, g, o, logs, q_label, k_label, base, far):
    rows, total, width, far_len = q.shape[0], k.shape[0], base.shape[2], far.shape[3]
    s = attention_specs(rows, total, width, far_len)
    return pl.pallas_call(
        backward_kernel,
        grid=(PAIRS,),
        in_specs=[
            s["q"], s["k"], s["k"], s["q"], s["q"], s["log"],
            s["q_label"], s["k_label"], s["base"], s["far"],
        ],
        out_specs=[s["q"], s["k"], s["k"], s["diag"], s["far"]],
        out_shape=[
            jax.ShapeDtypeStruct((rows, PAIRS * LANES), jnp.bfloat16),
            jax.ShapeDtypeStruct((total, PAIRS * LANES), jnp.bfloat16),
            jax.ShapeDtypeStruct((total, PAIRS * LANES), jnp.bfloat16),
            jax.ShapeDtypeStruct((PAIRS, 2, 8, width), jnp.float32),
            jax.ShapeDtypeStruct((PAIRS, 2, rows // GB, far_len), jnp.float32),
        ],
        scratch_shapes=[
            pltpu.VMEM((LANES, width), jnp.float32),
            pltpu.VMEM((rows, total), jnp.float32),
            pltpu.VMEM((rows, total), jnp.float32),
            pltpu.VMEM((2 * rows, total), jnp.bfloat16),
            pltpu.VMEM((2 * rows, total), jnp.bfloat16),
            pltpu.VMEM((LANES, width), jnp.float32),
            pltpu.VMEM((2, rows, LANES), jnp.float32),
            pltpu.VMEM((2 * rows, LANES), jnp.bfloat16),
            pltpu.VMEM((2 * rows, LANES), jnp.bfloat16),
        ],
        compiler_params=pltpu.CompilerParams(vmem_limit_bytes=VMEM_LIMIT),
        name="attention_backward",
    )(q, k, v, g, o, logs, q_label, k_label, base, far)


def on_device(
    hidden, cotangent, query_proj, key_proj, value_proj, out_proj, gate_proj, up_proj,
    down_proj, first_gain, second_gain, global_gain, local_bias, side_bias,
    segments, local_buckets, global_buckets,
):
    x_own = hidden[0]
    cot = cotangent[0]
    rows, width = x_own.shape
    cycle_size = lax.axis_size(CTX)
    cycle_index = lax.axis_index(CTX)
    first_row = cycle_index * rows
    far_len = rows * cycle_size // GB
    own_blocks = rows // GB
    reach = HALF // rows
    near_len = rows + 2 * HALF

    left = [shifted(x_own, CTX, d) for d in range(reach, 0, -1)]
    right = [shifted(x_own, CTX, -d) for d in range(1, reach + 1)]
    window = jnp.concatenate(left + [x_own] + right, axis=0)

    gather = lambda a: lax.all_gather(a, SHARD, axis=0, tiled=True)
    whole = lambda a: a.reshape(-1, a.shape[-1])
    first_set = gather(jnp.stack([query_proj, key_proj, value_proj, out_proj])[None])
    w_query, w_key, w_value, w_out = [whole(first_set[:, i]) for i in range(4)]
    second_set = gather(jnp.stack([gate_proj, up_proj])[None])
    w_gate, w_up = [whole(second_set[:, i]) for i in range(2)]
    w_down = gather(down_proj)
    small = jnp.concatenate(
        [first_gain, second_gain, global_gain, local_bias.reshape(-1), side_bias.reshape(-1)]
    )
    small = gather(small[None])
    cut = first_gain.shape[0]
    gain_one = small[:, :cut].reshape(-1).astype(jnp.float32)
    gain_two = small[:, cut : 2 * cut].reshape(-1).astype(jnp.float32)
    gain_side = small[:, 2 * cut : 3 * cut].reshape(-1).astype(jnp.float32)
    tab = local_bias.size
    near_tab = small[:, 3 * cut : 3 * cut + tab].reshape(NB, H)
    side_tab = small[:, 3 * cut + tab :].reshape(NB, H)

    bucket_iota = jnp.arange(NB, dtype=jnp.int32)[None, :]
    onehot_near = (local_buckets[:, None] == bucket_iota).astype(jnp.bfloat16)
    near_row = lax.dot_general(
        near_tab, onehot_near, (((0,), (1,)), ((), ())), preferred_element_type=jnp.float32
    )
    table_width = near_len + LANES
    base = jnp.pad(
        near_row,
        ((0, 0), (LANES + 1, table_width - LANES - 1 - near_row.shape[1])),
        constant_values=NEG,
    ).reshape(PAIRS, 2, table_width)
    far_start = far_len - own_blocks - cycle_index * own_blocks
    bucket_slice = lax.dynamic_slice_in_dim(global_buckets, far_start, far_len + own_blocks - 1, 0)
    onehot_side = (bucket_slice[:, None] == bucket_iota).astype(jnp.bfloat16)
    side_row = lax.dot_general(
        side_tab, onehot_side, (((0,), (1,)), ((), ())), preferred_element_type=jnp.float32
    )
    far = jnp.stack(
        [side_row[:, own_blocks - 1 - r : own_blocks - 1 - r + far_len] for r in range(own_blocks)],
        axis=1,
    ).reshape(PAIRS, 2, own_blocks, far_len)
    labels = segments[0]
    label_iota = jnp.arange(LANES, dtype=jnp.int32)[None, :]
    label_query = lax.dynamic_slice_in_dim(labels, first_row, rows, 0)
    label_pad = jnp.pad(labels, (HALF, HALF), constant_values=-1)
    label_window = lax.dynamic_slice_in_dim(label_pad, first_row, near_len, 0)
    label_keys = jnp.concatenate([label_window, labels[::GB]])
    q_label = (label_query[:, None] == label_iota).astype(jnp.bfloat16)
    k_label = jnp.where(label_keys[:, None] == label_iota, 0.0, NEG).astype(jnp.bfloat16)

    wide = window.astype(jnp.float32)
    scale_wide = rms_scale(wide)
    normed_wide = ((wide * scale_wide) * gain_one).astype(jnp.bfloat16)
    inputs = x_own.astype(jnp.float32)
    scale_one = rms_scale(inputs)
    normed_one = inputs * scale_one
    normed = (normed_one * gain_one).astype(jnp.bfloat16)
    block_sums = jnp.sum(normed.astype(jnp.float32).reshape(own_blocks, GB, width), axis=1)
    scale_side = rms_scale(block_sums)
    normed_side = block_sums * scale_side
    side_rows = (normed_side * gain_side).astype(jnp.bfloat16)
    all_rows = gather_over(gather_over(side_rows, "y", [1]), "z", bits("z"))
    key_rows = jnp.concatenate([normed_wide, all_rows], axis=0)
    queries = dot_nn(normed, w_query).astype(jnp.bfloat16)
    keys = dot_nn(key_rows, w_key).astype(jnp.bfloat16)
    values = dot_nn(key_rows, w_value).astype(jnp.bfloat16)
    attended, logs = attention_forward(queries, keys, values, q_label, k_label, base, far)
    middle = inputs + dot_nn(attended, w_out)
    scale_two = rms_scale(middle)
    normed_two = middle * scale_two
    ffn_in = (normed_two * gain_two).astype(jnp.bfloat16)
    gate_pre = dot_nn(ffn_in, w_gate)
    up_pre = dot_nn(ffn_in, w_up)
    gelu_out, gelu_pull = jax.vjp(lambda v: jax.nn.gelu(v, approximate=True), gate_pre)
    product = (gelu_out * up_pre).astype(jnp.bfloat16)
    outputs = (middle + dot_nn(product, w_down)).astype(jnp.bfloat16)

    down_grad = dot_tn(product, cot)
    product_grad = dot_nt(cot, w_down)
    gate_delta = gelu_pull(product_grad * up_pre)[0].astype(jnp.bfloat16)
    up_delta = (product_grad * gelu_out).astype(jnp.bfloat16)
    gate_grad = dot_tn(ffn_in, gate_delta)
    up_grad = dot_tn(ffn_in, up_delta)
    ffn_back = dot_nt(gate_delta, w_gate) + dot_nt(up_delta, w_up)
    second_part = jnp.sum(ffn_back * normed_two, axis=0)
    middle_grad = cot.astype(jnp.float32) + norm_back(ffn_back, normed_two, scale_two, gain_two)
    mixed_grad = middle_grad.astype(jnp.bfloat16)
    out_grad = dot_tn(attended, mixed_grad)
    attended_grad = dot_nt(mixed_grad, w_out).astype(jnp.bfloat16)

    dq, dk, dv, diag, dfar = attention_backward(
        queries, keys, values, attended_grad, attended, logs, q_label, k_label, base, far
    )
    far_back = dot_nt(dk[near_len:], w_key) + dot_nt(dv[near_len:], w_value)
    side_back = scatter_over(far_back.astype(jnp.bfloat16), "z", bits("z")[::-1])
    side_back = scatter_over(side_back, "y", [1]).astype(jnp.float32)
    query_grad = dot_tn(normed, dq)
    key_grad = dot_tn(key_rows, dk)
    value_grad = dot_tn(key_rows, dv)
    key_back = dot_nt(dk[:near_len], w_key) + dot_nt(dv[:near_len], w_value)
    own_start = reach * rows
    normed_back = dot_nt(dq, w_query) + key_back[own_start : own_start + rows]
    back_low = key_back.astype(jnp.bfloat16)
    for distance in range(1, reach + 1):
        for direction in (1, -1):
            at = (reach - direction * distance) * rows
            normed_back = normed_back + shifted(
                back_low[at : at + rows], CTX, -direction * distance
            ).astype(jnp.float32)
    global_part = jnp.sum(side_back * normed_side, axis=0)
    sums_grad = norm_back(side_back, normed_side, scale_side, gain_side)
    normed_back = (
        normed_back.reshape(own_blocks, GB, width) + sums_grad[:, None, :]
    ).reshape(rows, width)
    first_part = jnp.sum(normed_back * normed_one, axis=0)
    hidden_grad = (
        middle_grad + norm_back(normed_back, normed_one, scale_one, gain_one)
    ).astype(jnp.bfloat16)

    diag = diag.reshape(H, 8, table_width)
    near_sum = diag[:, 0]
    for r in range(1, 8):
        near_sum = near_sum + jnp.roll(diag[:, r], -r, axis=1)
    near_sum = near_sum[:, LANES + 1 : LANES + 2 * HALF]
    local_part = lax.dot_general(
        onehot_near.astype(jnp.float32), near_sum, (((0,), (1,)), ((), ())), precision=HIGHEST
    )
    dfar = dfar.reshape(H, own_blocks, far_len)
    side_sum = sum(
        jnp.pad(dfar[:, r], ((0, 0), (own_blocks - 1 - r, r))) for r in range(own_blocks)
    )
    side_part = lax.dot_general(
        onehot_side.astype(jnp.float32), side_sum, (((0,), (1,)), ((), ())), precision=HIGHEST
    )

    cut, deep = query_proj.shape[0], down_proj.shape[0]
    plane = lambda a: lax.psum_scatter(a, ("x", "y"), scatter_dimension=0, tiled=True)
    (down_sum,) = core_sums([down_grad], [deep])
    down_sum = over_lines(plane(whole(down_sum)))
    pair = jnp.stack(core_sums([gate_grad, up_grad], [cut] * 2), axis=1)
    pair = over_lines(plane(whole(pair))).reshape(2, cut, -1)
    four = jnp.stack(core_sums([query_grad, key_grad, value_grad, out_grad], [cut] * 4), axis=1)
    four = over_lines(scatter_planes(four.reshape(2, 2, 2 * cut, -1))).reshape(4, cut, -1)
    big = [four[0], four[1], four[2], four[3], pair[0], pair[1], down_sum]
    big = [a.astype(jnp.float32) for a in big]
    tiny = jnp.concatenate(
        [a.reshape(-1) for a in (first_part, second_part, global_part, local_part, side_part)]
    ).reshape(-1, LANES)
    for axis in ("c", "x", "y", "z"):
        for bit in bits(axis):
            tiny = tiny + swapped(tiny, axis, bit)
    tiny = tiny.reshape(-1)
    shard = lax.axis_index(SHARD)
    done, at = [], 0
    for a in (first_part, second_part, global_part, local_part, side_part):
        whole_sum = tiny[at : at + a.size].reshape(a.shape)
        at += a.size
        part = a.shape[0] // lax.axis_size(SHARD)
        done.append(lax.dynamic_slice_in_dim(whole_sum, shard * part, part, 0))
    return (outputs[None], hidden_grad[None], *big, *done)


def solution(mesh):
    ctx, shard = mesh.shape["ctx"], mesh.shape["shard"]
    fine = jax.sharding.Mesh(
        mesh.devices.reshape(ctx // 2, 2, shard // 2, 2), CTX + SHARD
    )
    tokens = P(SHARD, CTX, None)
    weight = P(SHARD, None)
    gain = P(SHARD)
    return jax.shard_map(
        on_device,
        mesh=fine,
        in_specs=(tokens, tokens) + (weight,) * 7 + (gain,) * 3 + (weight,) * 3 + (P(), P()),
        out_specs=(tokens, tokens) + (weight,) * 7 + (gain,) * 3 + (weight,) * 2,
        check_vma=False,
    )
```

```python
import jax
import jax.numpy as jnp
from jax import lax
from jax.experimental import pallas as pl
from jax.experimental.pallas import tpu as pltpu
from jax.sharding import PartitionSpec as P

H = 12
HD = 64
NB = 32
GB = 16
HALF = 512
LANES = 128
PAIRS = H * HD // LANES

EPS = 1e-06
NEG = -1e30
HIGHEST = lax.Precision.HIGHEST
VMEM_LIMIT = 60 << 20


CTX = ("z", "y")
SHARD = ("x", "c")


def shifted(value, axis, by):
    length = lax.axis_size(axis)
    pairs = [(i, i + by) for i in range(length) if 0 <= i + by < length]
    return lax.ppermute(value, axis, pairs)


def swapped(value, axis, bit=1):
    return lax.ppermute(value, axis, [(i, i ^ bit) for i in range(lax.axis_size(axis))])


def pick(value, index, dim=0):
    return lax.dynamic_index_in_dim(value, index, dim, keepdims=False)


def bit_of(axis, bit):
    return (lax.axis_index(axis) // bit) % 2


def halves(value):
    return value.reshape(2, value.shape[0] // 2, *value.shape[1:])


def in_order(own, other, upper, dim=0):
    return jnp.where(
        upper == 1,
        jnp.concatenate([other, own], axis=dim),
        jnp.concatenate([own, other], axis=dim),
    )


def add_low(left, right):
    return (left.astype(jnp.float32) + right.astype(jnp.float32)).astype(jnp.bfloat16)


def bits(axis):
    return [1 << k for k in range(lax.axis_size(axis).bit_length() - 1)]


def scatter_over(value, axis, order):
    for bit in order:
        both, mine = halves(value), bit_of(axis, bit)
        value = add_low(pick(both, mine), swapped(pick(both, 1 - mine), axis, bit))
    return value


def gather_over(value, axis, order):
    for bit in order:
        value = in_order(value, swapped(value, axis, bit), bit_of(axis, bit))
    return value


def fence(*values):
    return lax.optimization_barrier(values)


def core_sums(grads, rows):
    core = lax.axis_index("c")
    split = [a.astype(jnp.bfloat16).reshape(2, 2, r, a.shape[1]) for a, r in zip(grads, rows)]
    got = [swapped(pick(a, 1 - core, 1), "c") for a in split]
    return [add_low(pick(a, core, 1), b) for a, b in zip(split, got)]


def pair_first(one, two):
    x, y = lax.axis_index("x"), lax.axis_index("y")
    two = two.reshape(2, 2, two.shape[1] // 2, two.shape[2])
    got_one = swapped(pick(one, 1 - x), "x")
    got_two = swapped(pick(two, 1 - y, 1), "y")
    return add_low(pick(one, x), got_one), add_low(pick(two, y, 1), got_two)


def pair_second(one, two):
    x, y = lax.axis_index("x"), lax.axis_index("y")
    one = halves(one)
    got_one = swapped(pick(one, 1 - y), "y")
    got_two = swapped(pick(two, 1 - x), "x")
    one = add_low(pick(one, y), got_one)
    two = add_low(pick(two, x), got_two)
    return jnp.concatenate([one, two], axis=0)


def dot_nn(left, right):
    return lax.dot_general(
        left, right, (((1,), (0,)), ((), ())), preferred_element_type=jnp.float32
    )


def dot_nt(left, right):
    return lax.dot_general(
        left, right, (((1,), (1,)), ((), ())), preferred_element_type=jnp.float32
    )


def dot_tn(left, right):
    return lax.dot_general(
        left, right, (((0,), (0,)), ((), ())), preferred_element_type=jnp.float32
    )


def rms_scale(values):
    return lax.rsqrt(jnp.mean(values * values, axis=-1, keepdims=True) + EPS)


def norm_back(upstream, normed_val, row_scale, gain_row):
    scaled = upstream * gain_row
    return row_scale * (scaled - normed_val * jnp.mean(scaled * normed_val, axis=-1, keepdims=True))


def head_mask(head):
    lane = lax.broadcasted_iota(jnp.int32, (1, LANES), 1)
    own = (lane < HD) if head == 0 else (lane >= HD)
    return own.astype(jnp.float32)


def fill_offsets(base_ref, head, table_ref):
    width = table_ref.shape[1]
    base = jnp.broadcast_to(base_ref[0, head : head + 1, :], (8, width))
    base = pltpu.roll(base, 0, 1, stride=1, stride_axis=0)
    for group in range(LANES // 8):
        table_ref[group * 8 : group * 8 + 8, :] = (
            pltpu.roll(base, group * 8, 1) if group else base
        )


def score_rows(score_ref, table_ref, far_ref, head, half, step, near_len):
    row = pl.multiple_of(half * LANES + step * GB, GB)
    start = LANES if half == 0 else 0
    bias = table_ref[pl.ds(pl.multiple_of(step * GB, GB), GB), start : start + near_len]
    near = score_ref[pl.ds(row, GB), :near_len] + bias
    far = score_ref[pl.ds(row, GB), near_len:] + far_ref[
        0, head, pl.ds(half * (LANES // GB) + step, 1), :
    ]
    return row, near, far


def forward_kernel(
    q_ref, k_ref, v_ref, q_label_ref, k_label_ref, base_ref, far_ref,
    out_ref, log_ref,
    table_ref, score_ref, prob_ref, total_ref,
):
    rows = q_ref.shape[0]
    near_len = table_ref.shape[1] - LANES
    keys = jnp.concatenate([k_ref[...], k_label_ref[...]], axis=1)
    out = None
    logs = None
    for head in range(2):
        mask = head_mask(head)
        query = jnp.concatenate(
            [q_ref[...] * mask.astype(jnp.bfloat16), q_label_ref[...]], axis=1
        )
        score_ref[...] = dot_nt(query, keys)
        fill_offsets(base_ref, head, table_ref)
        for half in range(rows // LANES):

            def body(step, carry, half=half, head=head):
                row, near, far = score_rows(
                    score_ref, table_ref, far_ref, head, half, step, near_len
                )
                peak = jnp.maximum(
                    jnp.max(near, axis=1, keepdims=True), jnp.max(far, axis=1, keepdims=True)
                )
                near = jnp.exp(near - peak)
                far = jnp.exp(far - peak)
                total = jnp.sum(near, axis=1, keepdims=True) + jnp.sum(far, axis=1, keepdims=True)
                prob_ref[pl.ds(row, GB), :near_len] = near.astype(jnp.bfloat16)
                prob_ref[pl.ds(row, GB), near_len:] = far.astype(jnp.bfloat16)
                total_ref[0, pl.ds(row, GB), :] = jnp.broadcast_to(total, (GB, LANES))
                total_ref[1, pl.ds(row, GB), :] = jnp.broadcast_to(
                    peak + jnp.log(total), (GB, LANES)
                )
                return carry

            lax.fori_loop(0, LANES // GB, body, 0, unroll=2)
        mixed = dot_nn(prob_ref[...], v_ref[...]) / total_ref[0] * mask
        out = mixed if out is None else out + mixed
        part = total_ref[1] * mask
        logs = part if logs is None else logs + part
    out_ref[...] = out.astype(jnp.bfloat16)
    log_ref[0] = logs


def backward_kernel(
    q_ref, k_ref, v_ref, g_ref, o_ref, log_ref, q_label_ref, k_label_ref, base_ref, far_ref,
    dq_ref, dk_ref, dv_ref, diag_ref, dfar_ref,
    table_ref, score_ref, dprob_ref, prob_ref, delta_ref, fold_ref, col_ref, q_two, g_two,
):
    rows = q_ref.shape[0]
    near_len = table_ref.shape[1] - LANES
    keys = jnp.concatenate([k_ref[...], k_label_ref[...]], axis=1)
    weighted = g_ref[...].astype(jnp.float32) * o_ref[...].astype(jnp.float32)
    for head in range(2):
        mask = head_mask(head)
        mask_low = mask.astype(jnp.bfloat16)
        own_q = q_ref[...] * mask_low
        own_g = g_ref[...] * mask_low
        q_two[head * rows : (head + 1) * rows, :] = own_q
        g_two[head * rows : (head + 1) * rows, :] = own_g
        query = jnp.concatenate([own_q, q_label_ref[...]], axis=1)
        score_ref[...] = dot_nt(query, keys)
        dprob_ref[...] = dot_nt(own_g, v_ref[...])
        fill_offsets(base_ref, head, table_ref)
        col_ref[0] = jnp.broadcast_to(
            jnp.sum(weighted * mask, axis=1, keepdims=True), (rows, LANES)
        )
        col_ref[1] = jnp.broadcast_to(
            log_ref[0, :, head * HD : head * HD + 1], (rows, LANES)
        )
        for half in range(rows // LANES):

            def body(step, carry, half=half, head=head):
                row, near, far = score_rows(
                    score_ref, table_ref, far_ref, head, half, step, near_len
                )
                center = col_ref[0, pl.ds(row, GB), 0:1]
                logs = col_ref[1, pl.ds(row, GB), 0:1]
                to_row = pl.multiple_of(head * rows + row, GB)
                near = jnp.exp(near - logs)
                far = jnp.exp(far - logs)
                prob_ref[pl.ds(to_row, GB), :near_len] = near.astype(jnp.bfloat16)
                prob_ref[pl.ds(to_row, GB), near_len:] = far.astype(jnp.bfloat16)
                near = near * (dprob_ref[pl.ds(row, GB), :near_len] - center)
                far = far * (dprob_ref[pl.ds(row, GB), near_len:] - center)
                delta_ref[pl.ds(to_row, GB), :near_len] = near.astype(jnp.bfloat16)
                delta_ref[pl.ds(to_row, GB), near_len:] = far.astype(jnp.bfloat16)
                at = pl.ds(pl.multiple_of(step * GB, GB), GB)
                if half == 0:
                    fold_ref[at, :LANES] = jnp.zeros((GB, LANES), jnp.float32)
                    fold_ref[at, LANES:] = near
                else:
                    fold_ref[at, :near_len] += near
                dfar_ref[0, head, pl.ds(half * (LANES // GB) + step, 1), :] = jnp.sum(
                    far, axis=0, keepdims=True
                )
                return carry

            lax.fori_loop(0, LANES // GB, body, 0, unroll=2)
        diag = fold_ref[0:8, :]
        width = table_ref.shape[1]
        for group in range(1, LANES // 8):
            diag = diag + pltpu.roll(fold_ref[group * 8 : group * 8 + 8, :], width - group * 8, 1)
        diag_ref[0, head] = diag
    low = dot_nn(delta_ref[:rows, :], k_ref[...]) * head_mask(0)
    high = dot_nn(delta_ref[rows:, :], k_ref[...]) * head_mask(1)
    dq_ref[...] = (low + high).astype(jnp.bfloat16)
    dk_ref[...] = dot_tn(q_two[...], delta_ref[...]).T.astype(jnp.bfloat16)
    dv_ref[...] = dot_tn(g_two[...], prob_ref[...]).T.astype(jnp.bfloat16)


def kernel_cost(rows, total):
    return pl.CostEstimate(
        flops=rows * total * PAIRS * LANES * 120, transcendentals=0, bytes_accessed=1 << 20
    )


def attention_specs(rows, total, width, far_len):
    col = lambda p: (0, p)
    return dict(
        q=pl.BlockSpec((rows, LANES), col),
        k=pl.BlockSpec((total, LANES), col),
        q_label=pl.BlockSpec((rows, LANES), lambda p: (0, 0)),
        k_label=pl.BlockSpec((total, LANES), lambda p: (0, 0)),
        base=pl.BlockSpec((1, 2, width), lambda p: (p, 0, 0)),
        far=pl.BlockSpec((1, 2, rows // GB, far_len), lambda p: (p, 0, 0, 0)),
        log=pl.BlockSpec((1, rows, LANES), lambda p: (p, 0, 0)),
        diag=pl.BlockSpec((1, 2, 8, width), lambda p: (p, 0, 0, 0)),
    )


def attention_forward(q, k, v, q_label, k_label, base, far):
    rows, total, width, far_len = q.shape[0], k.shape[0], base.shape[2], far.shape[3]
    s = attention_specs(rows, total, width, far_len)
    return pl.pallas_call(
        forward_kernel,
        grid=(PAIRS,),
        in_specs=[s["q"], s["k"], s["k"], s["q_label"], s["k_label"], s["base"], s["far"]],
        out_specs=[s["q"], s["log"]],
        out_shape=[
            jax.ShapeDtypeStruct((rows, PAIRS * LANES), jnp.bfloat16),
            jax.ShapeDtypeStruct((PAIRS, rows, LANES), jnp.float32),
        ],
        scratch_shapes=[
            pltpu.VMEM((LANES, width), jnp.float32),
            pltpu.VMEM((rows, total), jnp.float32),
            pltpu.VMEM((rows, total), jnp.bfloat16),
            pltpu.VMEM((2, rows, LANES), jnp.float32),
        ],
        compiler_params=pltpu.CompilerParams(vmem_limit_bytes=VMEM_LIMIT),
        cost_estimate=kernel_cost(rows, total),
        name="attention_forward",
    )(q, k, v, q_label, k_label, base, far)


def attention_backward(q, k, v, g, o, logs, q_label, k_label, base, far):
    rows, total, width, far_len = q.shape[0], k.shape[0], base.shape[2], far.shape[3]
    s = attention_specs(rows, total, width, far_len)
    return pl.pallas_call(
        backward_kernel,
        grid=(PAIRS,),
        in_specs=[
            s["q"], s["k"], s["k"], s["q"], s["q"], s["log"],
            s["q_label"], s["k_label"], s["base"], s["far"],
        ],
        out_specs=[s["q"], s["k"], s["k"], s["diag"], s["far"]],
        out_shape=[
            jax.ShapeDtypeStruct((rows, PAIRS * LANES), jnp.bfloat16),
            jax.ShapeDtypeStruct((total, PAIRS * LANES), jnp.bfloat16),
            jax.ShapeDtypeStruct((total, PAIRS * LANES), jnp.bfloat16),
            jax.ShapeDtypeStruct((PAIRS, 2, 8, width), jnp.float32),
            jax.ShapeDtypeStruct((PAIRS, 2, rows // GB, far_len), jnp.float32),
        ],
        scratch_shapes=[
            pltpu.VMEM((LANES, width), jnp.float32),
            pltpu.VMEM((rows, total), jnp.float32),
            pltpu.VMEM((rows, total), jnp.float32),
            pltpu.VMEM((2 * rows, total), jnp.bfloat16),
            pltpu.VMEM((2 * rows, total), jnp.bfloat16),
            pltpu.VMEM((LANES, width), jnp.float32),
            pltpu.VMEM((2, rows, LANES), jnp.float32),
            pltpu.VMEM((2 * rows, LANES), jnp.bfloat16),
            pltpu.VMEM((2 * rows, LANES), jnp.bfloat16),
        ],
        compiler_params=pltpu.CompilerParams(vmem_limit_bytes=VMEM_LIMIT),
        cost_estimate=kernel_cost(rows, total),
        name="attention_backward",
    )(q, k, v, g, o, logs, q_label, k_label, base, far)


def on_device(
    hidden, cotangent, query_proj, key_proj, value_proj, out_proj, gate_proj, up_proj,
    down_proj, first_gain, second_gain, global_gain, local_bias, side_bias,
    segments, local_buckets, global_buckets,
):
    x_own = hidden[0]
    cot = cotangent[0]
    rows, width = x_own.shape
    cycle_size = lax.axis_size(CTX)
    cycle_index = lax.axis_index(CTX)
    first_row = cycle_index * rows
    far_len = rows * cycle_size // GB
    own_blocks = rows // GB
    reach = HALF // rows
    near_len = rows + 2 * HALF

    left = [shifted(x_own, CTX, d) for d in range(reach, 0, -1)]
    right = [shifted(x_own, CTX, -d) for d in range(1, reach + 1)]
    window = jnp.concatenate(left + [x_own] + right, axis=0)

    gather = lambda a: lax.all_gather(a, SHARD, axis=0, tiled=True)
    whole = lambda a: a.reshape(-1, a.shape[-1])
    first_set = gather(jnp.stack([query_proj, key_proj, value_proj, out_proj])[None])
    first_set, down_part = fence(first_set, pick(halves(down_proj), lax.axis_index("y")))
    from_x = swapped(down_part, "x")
    w_query, w_key, w_value, w_out = [whole(first_set[:, i]) for i in range(4)]
    second_set = gather(jnp.stack([gate_proj, up_proj])[None])
    w_gate, w_up = [whole(second_set[:, i]) for i in range(2)]
    small = jnp.concatenate(
        [first_gain, second_gain, global_gain, local_bias.reshape(-1), side_bias.reshape(-1)]
    )
    small = gather(small[None])
    cut = first_gain.shape[0]
    gain_one = small[:, :cut].reshape(-1).astype(jnp.float32)
    gain_two = small[:, cut : 2 * cut].reshape(-1).astype(jnp.float32)
    gain_side = small[:, 2 * cut : 3 * cut].reshape(-1).astype(jnp.float32)
    tab = local_bias.size
    near_tab = small[:, 3 * cut : 3 * cut + tab].reshape(NB, H)
    side_tab = small[:, 3 * cut + tab :].reshape(NB, H)

    bucket_iota = jnp.arange(NB, dtype=jnp.int32)[None, :]
    onehot_near = (local_buckets[:, None] == bucket_iota).astype(jnp.bfloat16)
    near_row = lax.dot_general(
        near_tab, onehot_near, (((0,), (1,)), ((), ())), preferred_element_type=jnp.float32
    )
    table_width = near_len + LANES
    base = jnp.pad(
        near_row,
        ((0, 0), (LANES + 1, table_width - LANES - 1 - near_row.shape[1])),
        constant_values=NEG,
    ).reshape(PAIRS, 2, table_width)
    far_start = far_len - own_blocks - cycle_index * own_blocks
    bucket_slice = lax.dynamic_slice_in_dim(global_buckets, far_start, far_len + own_blocks - 1, 0)
    onehot_side = (bucket_slice[:, None] == bucket_iota).astype(jnp.bfloat16)
    side_row = lax.dot_general(
        side_tab, onehot_side, (((0,), (1,)), ((), ())), preferred_element_type=jnp.float32
    )
    far = jnp.stack(
        [side_row[:, own_blocks - 1 - r : own_blocks - 1 - r + far_len] for r in range(own_blocks)],
        axis=1,
    ).reshape(PAIRS, 2, own_blocks, far_len)
    labels = segments[0]
    label_iota = jnp.arange(LANES, dtype=jnp.int32)[None, :]
    label_query = lax.dynamic_slice_in_dim(labels, first_row, rows, 0)
    label_pad = jnp.pad(labels, (HALF, HALF), constant_values=-1)
    label_window = lax.dynamic_slice_in_dim(label_pad, first_row, near_len, 0)
    label_keys = jnp.concatenate([label_window, labels[::GB]])
    q_label = (label_query[:, None] == label_iota).astype(jnp.bfloat16)
    k_label = jnp.where(label_keys[:, None] == label_iota, 0.0, NEG).astype(jnp.bfloat16)

    wide = window.astype(jnp.float32)
    scale_wide = rms_scale(wide)
    normed_wide = ((wide * scale_wide) * gain_one).astype(jnp.bfloat16)
    inputs = x_own.astype(jnp.float32)
    scale_one = rms_scale(inputs)
    normed_one = inputs * scale_one
    normed = (normed_one * gain_one).astype(jnp.bfloat16)
    block_sums = jnp.sum(normed.astype(jnp.float32).reshape(own_blocks, GB, width), axis=1)
    scale_side = rms_scale(block_sums)
    normed_side = block_sums * scale_side
    side_rows = (normed_side * gain_side).astype(jnp.bfloat16)
    all_rows = gather_over(gather_over(side_rows, "y", [1]), "z", bits("z"))
    key_rows = jnp.concatenate([normed_wide, all_rows], axis=0)
    queries = dot_nn(normed, w_query).astype(jnp.bfloat16)
    keys = dot_nn(key_rows, w_key).astype(jnp.bfloat16)
    values = dot_nn(key_rows, w_value).astype(jnp.bfloat16)
    queries, keys, values = fence(queries, keys, values)
    attended, logs = attention_forward(queries, keys, values, q_label, k_label, base, far)
    attended, logs, from_x = fence(attended, logs, from_x)
    from_y = swapped(from_x, "y")
    middle = inputs + dot_nn(attended, w_out)
    scale_two = rms_scale(middle)
    normed_two = middle * scale_two
    ffn_in = (normed_two * gain_two).astype(jnp.bfloat16)
    ffn_in, from_y = fence(ffn_in, from_y)
    pair = in_order(from_x, from_y, lax.axis_index("y"))
    pair = in_order(down_proj[None], pair[None], lax.axis_index("x"))
    other = swapped(pair, "c")
    gate_pre = dot_nn(ffn_in, w_gate)
    up_pre = dot_nn(ffn_in, w_up)
    gate_pre, up_pre, other = fence(gate_pre, up_pre, other)
    w_down = whole(in_order(pair[:, None], other[:, None], lax.axis_index("c"), 1))
    gelu_out, gelu_pull = jax.vjp(lambda v: jax.nn.gelu(v, approximate=True), gate_pre)
    product = (gelu_out * up_pre).astype(jnp.bfloat16)
    outputs = (middle + dot_nn(product, w_down)).astype(jnp.bfloat16)

    down_grad = dot_tn(product, cot)
    product_grad = dot_nt(cot, w_down)
    gate_delta = gelu_pull(product_grad * up_pre)[0].astype(jnp.bfloat16)
    up_delta = (product_grad * gelu_out).astype(jnp.bfloat16)
    gate_grad = dot_tn(ffn_in, gate_delta)
    up_grad = dot_tn(ffn_in, up_delta)
    ffn_back = dot_nt(gate_delta, w_gate) + dot_nt(up_delta, w_up)
    second_part = jnp.sum(ffn_back * normed_two, axis=0)
    middle_grad = cot.astype(jnp.float32) + norm_back(ffn_back, normed_two, scale_two, gain_two)
    mixed_grad = middle_grad.astype(jnp.bfloat16)
    out_grad = dot_tn(attended, mixed_grad)
    attended_grad = dot_nt(mixed_grad, w_out).astype(jnp.bfloat16)

    cut, deep = query_proj.shape[0], down_proj.shape[0]
    plane = lambda a: lax.psum_scatter(a, ("x", "y"), scatter_dimension=0, tiled=True)
    down_sum = jnp.concatenate(core_sums([down_grad, out_grad], [deep, cut]), axis=1)
    pair = core_sums([gate_grad, up_grad], [cut] * 2)
    attended_grad, down_sum, pair = fence(attended_grad, whole(down_sum), pair)
    down_sum = plane(down_sum)
    pair = pair_first(*pair)

    dq, dk, dv, diag, dfar = attention_backward(
        queries, keys, values, attended_grad, attended, logs, q_label, k_label, base, far
    )
    up_z, down_z = bits("z"), bits("z")[::-1]
    near_z, rest_z = up_z[:1], up_z[1:]

    dq, dk, dv, diag, dfar, pair = fence(dq, dk, dv, diag, dfar, pair)
    pair = pair_second(*pair)
    far_back = dot_nt(dk[near_len:], w_key) + dot_nt(dv[near_len:], w_value)
    side_back = scatter_over(far_back.astype(jnp.bfloat16), "z", down_z[:-1])
    query_grad = dot_tn(normed, dq).astype(jnp.bfloat16)
    key_grad = dot_tn(key_rows, dk).astype(jnp.bfloat16)
    value_grad = dot_tn(key_rows, dv).astype(jnp.bfloat16)

    dq, dk, dv, query_grad, key_grad, value_grad, side_back, pair = fence(
        dq, dk, dv, query_grad, key_grad, value_grad, side_back, pair
    )
    three = jnp.concatenate(core_sums([query_grad, key_grad, value_grad], [cut] * 3), axis=1)
    pair = scatter_over(pair, "z", near_z)
    side_back = scatter_over(side_back, "z", down_z[-1:])
    key_back = dot_nt(dk[:near_len], w_key) + dot_nt(dv[:near_len], w_value)
    own_start = reach * rows
    normed_back = dot_nt(dq, w_query) + key_back[own_start : own_start + rows]
    back_low = key_back.astype(jnp.bfloat16)

    three, normed_back, back_low, side_back, pair, down_sum = fence(
        whole(three), normed_back, back_low, side_back, pair, down_sum
    )
    down_sum = scatter_over(down_sum, "z", near_z)
    three = scatter_over(three, "x", bits("x"))
    pair = scatter_over(pair, "z", rest_z)
    side_back = scatter_over(side_back, "y", [1]).astype(jnp.float32)
    low_y = lax.axis_index("y") == 0
    blocks = back_low.reshape(2 * reach + 1, rows, width)
    near_by = jnp.where(low_y, blocks[3], blocks[1])
    farther = jnp.where(low_y, blocks[1], blocks[3])
    got = swapped(jnp.stack([near_by, farther]), "y")

    three, got, side_back, normed_back, blocks, pair, down_sum = fence(
        three, got, side_back, normed_back, blocks, pair, down_sum
    )
    down_sum = scatter_over(down_sum, "z", rest_z)
    three = scatter_over(three, "y", [1])
    pair = gather_over(pair, "z", rest_z[::-1])
    zero = jnp.zeros_like(got[1])
    upward = shifted(add_low(blocks[4], jnp.where(low_y, got[1], zero)), "z", 1)
    downward = shifted(add_low(blocks[0], jnp.where(low_y, zero, got[1])), "z", -1)
    got = [got[0], upward, downward]
    global_part = jnp.sum(side_back * normed_side, axis=0)
    sums_grad = norm_back(side_back, normed_side, scale_side, gain_side)
    normed_back = (
        normed_back.reshape(own_blocks, GB, width) + sums_grad[:, None, :]
    ).reshape(rows, width)

    diag = diag.reshape(H, 8, table_width)
    near_sum = diag[:, 0]
    for r in range(1, 8):
        near_sum = near_sum + jnp.roll(diag[:, r], -r, axis=1)
    near_sum = near_sum[:, LANES + 1 : LANES + 2 * HALF]
    local_part = lax.dot_general(
        near_sum, onehot_near.astype(jnp.float32), (((1,), (0,)), ((), ())), precision=HIGHEST
    )
    dfar = dfar.reshape(H, own_blocks, far_len)
    side_sum = sum(
        jnp.pad(dfar[:, r], ((0, 0), (own_blocks - 1 - r, r))) for r in range(own_blocks)
    )
    side_part = lax.dot_general(
        side_sum, onehot_side.astype(jnp.float32), (((1,), (0,)), ((), ())), precision=HIGHEST
    )

    three, normed_back, got, local_part, side_part, global_part, pair, down_sum = fence(
        three, normed_back, got, local_part, side_part, global_part, pair, down_sum
    )
    three = scatter_over(three, "z", near_z)
    pair = gather_over(pair, "z", near_z)
    down_sum = gather_over(down_sum, "z", rest_z[::-1])
    for piece in got:
        normed_back = normed_back + piece.astype(jnp.float32)
    first_part = jnp.sum(normed_back * normed_one, axis=0)
    hidden_grad = (
        middle_grad + norm_back(normed_back, normed_one, scale_one, gain_one)
    ).astype(jnp.bfloat16)
    tables = jnp.concatenate([local_part, side_part], axis=0)
    tiny = jnp.concatenate(
        [
            jnp.stack([first_part, second_part, global_part]),
            jnp.pad(tables, ((0, 5), (0, width - tables.shape[1]))),
        ]
    )

    three, tiny, pair, down_sum = fence(three, tiny, pair, down_sum)
    three = scatter_over(three, "z", rest_z)
    pair = gather_over(pair, "y", [1])
    down_sum = gather_over(down_sum, "z", near_z)
    tiny = tiny + swapped(tiny, "c")
    tiny = tiny + swapped(tiny, "x")

    three, tiny, pair, down_sum = fence(three, tiny, pair, down_sum)
    three = gather_over(three, "z", rest_z[::-1])
    down_sum = gather_over(down_sum, "y", [1])
    tiny = tiny + swapped(tiny, "y")

    three, tiny, pair, down_sum = fence(three, tiny, pair, down_sum)
    three = gather_over(three, "z", near_z)
    for bit in near_z:
        tiny = tiny + swapped(tiny, "z", bit)

    three, tiny = fence(three, tiny)
    three = gather_over(three, "y", [1]).reshape(3, cut, -1)
    for bit in rest_z:
        tiny = tiny + swapped(tiny, "z", bit)
    pair = pair.reshape(2, 2, cut // 2, -1)
    pair = pair[:, 0].reshape(cut, -1), pair[:, 1].reshape(cut, -1)
    big = [three[0], three[1], three[2], down_sum[deep:], pair[0], pair[1], down_sum[:deep]]
    big = [a.astype(jnp.float32) for a in big]
    shards = lax.axis_size(SHARD)
    shard = lax.axis_index(SHARD)
    own = lax.dynamic_slice_in_dim(tiny[:3], shard * cut, cut, 1)
    bias_rows = NB // shards
    own_tables = lax.dynamic_slice_in_dim(tiny[3 : 3 + 2 * H, :NB], shard * bias_rows, bias_rows, 1).T
    done = [own[0], own[1], own[2], own_tables[:, :H], own_tables[:, H:]]
    return (outputs[None], hidden_grad[None], *big, *done)


def solution(mesh):
    ctx, shard = mesh.shape["ctx"], mesh.shape["shard"]
    fine = jax.sharding.Mesh(
        mesh.devices.reshape(ctx // 2, 2, shard // 2, 2), CTX + SHARD
    )
    tokens = P(SHARD, CTX, None)
    weight = P(SHARD, None)
    gain = P(SHARD)
    return jax.shard_map(
        on_device,
        mesh=fine,
        in_specs=(tokens, tokens) + (weight,) * 7 + (gain,) * 3 + (weight,) * 3 + (P(), P()),
        out_specs=(tokens, tokens) + (weight,) * 7 + (gain,) * 3 + (weight,) * 2,
        check_vma=False,
    )
```

```python
import jax
import jax.numpy as jnp
from jax import lax
from jax.experimental import pallas as pl
from jax.experimental.pallas import tpu as pltpu
from jax.sharding import PartitionSpec as P

H = 12
HD = 64
NB = 32
GB = 16
HALF = 512
LANES = 128
PAIRS = H * HD // LANES

EPS = 1e-06
NEG = -1e30
HIGHEST = lax.Precision.HIGHEST
VMEM_LIMIT = 20 << 20


CTX = ("z", "y")
SHARD = ("x", "c")


def shifted(value, axis, by):
    length = lax.axis_size(axis)
    pairs = [(i, i + by) for i in range(length) if 0 <= i + by < length]
    return lax.ppermute(value, axis, pairs)


def swapped(value, axis, bit=1):
    return lax.ppermute(value, axis, [(i, i ^ bit) for i in range(lax.axis_size(axis))])


def pick(value, index, dim=0):
    return lax.dynamic_index_in_dim(value, index, dim, keepdims=False)


def bit_of(axis, bit):
    return (lax.axis_index(axis) // bit) % 2


def halves(value):
    return value.reshape(2, value.shape[0] // 2, *value.shape[1:])


def in_order(own, other, upper, dim=0):
    return jnp.where(
        upper == 1,
        jnp.concatenate([other, own], axis=dim),
        jnp.concatenate([own, other], axis=dim),
    )


def add_low(left, right):
    return (left.astype(jnp.float32) + right.astype(jnp.float32)).astype(jnp.bfloat16)


def bits(axis):
    return [1 << k for k in range(lax.axis_size(axis).bit_length() - 1)]


def scatter_over(value, axis, order):
    for bit in order:
        both, mine = halves(value), bit_of(axis, bit)
        value = add_low(pick(both, mine), swapped(pick(both, 1 - mine), axis, bit))
    return value


def gather_over(value, axis, order):
    for bit in order:
        value = in_order(value, swapped(value, axis, bit), bit_of(axis, bit))
    return value


def fence(*values):
    return lax.optimization_barrier(values)


def core_sums(grads, rows):
    core = lax.axis_index("c")
    split = [a.astype(jnp.bfloat16).reshape(2, 2, r, a.shape[1]) for a, r in zip(grads, rows)]
    got = [swapped(pick(a, 1 - core, 1), "c") for a in split]
    return [add_low(pick(a, core, 1), b) for a, b in zip(split, got)]


def pair_first(one, two):
    x, y = lax.axis_index("x"), lax.axis_index("y")
    two = two.reshape(2, 2, two.shape[1] // 2, two.shape[2])
    got_one = swapped(pick(one, 1 - x), "x")
    got_two = swapped(pick(two, 1 - y, 1), "y")
    return add_low(pick(one, x), got_one), add_low(pick(two, y, 1), got_two)


def pair_second(one, two):
    x, y = lax.axis_index("x"), lax.axis_index("y")
    one = halves(one)
    got_one = swapped(pick(one, 1 - y), "y")
    got_two = swapped(pick(two, 1 - x), "x")
    one = add_low(pick(one, y), got_one)
    two = add_low(pick(two, x), got_two)
    return jnp.concatenate([one, two], axis=0)


def dot_nn(left, right):
    return lax.dot_general(
        left, right, (((1,), (0,)), ((), ())), preferred_element_type=jnp.float32
    )


def dot_nt(left, right):
    return lax.dot_general(
        left, right, (((1,), (1,)), ((), ())), preferred_element_type=jnp.float32
    )


def dot_tn(left, right):
    return lax.dot_general(
        left, right, (((0,), (0,)), ((), ())), preferred_element_type=jnp.float32
    )


def rms_scale(values):
    return lax.rsqrt(jnp.mean(values * values, axis=-1, keepdims=True) + EPS)


def norm_back(upstream, normed_val, row_scale, gain_row):
    scaled = upstream * gain_row
    return row_scale * (scaled - normed_val * jnp.mean(scaled * normed_val, axis=-1, keepdims=True))


def head_mask(head):
    lane = lax.broadcasted_iota(jnp.int32, (1, LANES), 1)
    own = (lane < HD) if head == 0 else (lane >= HD)
    return own.astype(jnp.float32)


def fill_offsets(base_ref, head, table_ref):
    width = table_ref.shape[1]
    base = jnp.broadcast_to(base_ref[0, head : head + 1, :], (8, width))
    base = pltpu.roll(base, 0, 1, stride=1, stride_axis=0)
    for group in range(LANES // 8):
        table_ref[group * 8 : group * 8 + 8, :] = (
            pltpu.roll(base, group * 8, 1) if group else base
        )


def score_rows(score_ref, table_ref, far_ref, head, half, step, near_len):
    row = pl.multiple_of(half * LANES + step * GB, GB)
    start = LANES if half == 0 else 0
    bias = table_ref[pl.ds(pl.multiple_of(step * GB, GB), GB), start : start + near_len]
    near = score_ref[pl.ds(row, GB), :near_len] + bias
    far = score_ref[pl.ds(row, GB), near_len:] + far_ref[
        0, head, pl.ds(half * (LANES // GB) + step, 1), :
    ]
    return row, near, far


def forward_kernel(
    q_ref, k_ref, v_ref, q_label_ref, k_label_ref, base_ref, far_ref,
    out_ref, log_ref,
    table_ref, score_ref, prob_ref, total_ref,
):
    rows = q_ref.shape[0]
    near_len = table_ref.shape[1] - LANES
    keys = jnp.concatenate([k_ref[...], k_label_ref[...]], axis=1)
    out = None
    logs = None
    for head in range(2):
        mask = head_mask(head)
        query = jnp.concatenate(
            [q_ref[...] * mask.astype(jnp.bfloat16), q_label_ref[...]], axis=1
        )
        score_ref[...] = dot_nt(query, keys)
        fill_offsets(base_ref, head, table_ref)
        for half in range(rows // LANES):

            def body(step, carry, half=half, head=head):
                row, near, far = score_rows(
                    score_ref, table_ref, far_ref, head, half, step, near_len
                )
                peak = jnp.maximum(
                    jnp.max(near, axis=1, keepdims=True), jnp.max(far, axis=1, keepdims=True)
                )
                near = jnp.exp(near - peak)
                far = jnp.exp(far - peak)
                total = jnp.sum(near, axis=1, keepdims=True) + jnp.sum(far, axis=1, keepdims=True)
                prob_ref[pl.ds(row, GB), :near_len] = near.astype(jnp.bfloat16)
                prob_ref[pl.ds(row, GB), near_len:] = far.astype(jnp.bfloat16)
                total_ref[0, pl.ds(row, GB), :] = jnp.broadcast_to(total, (GB, LANES))
                total_ref[1, pl.ds(row, GB), :] = jnp.broadcast_to(
                    peak + jnp.log(total), (GB, LANES)
                )
                return carry

            lax.fori_loop(0, LANES // GB, body, 0, unroll=2)
        mixed = dot_nn(prob_ref[...], v_ref[...]) / total_ref[0] * mask
        out = mixed if out is None else out + mixed
        part = total_ref[1] * mask
        logs = part if logs is None else logs + part
    out_ref[...] = out.astype(jnp.bfloat16)
    log_ref[0] = logs


def backward_kernel(
    q_ref, k_ref, v_ref, g_ref, o_ref, log_ref, q_label_ref, k_label_ref, base_ref, far_ref,
    dq_ref, dk_ref, dv_ref, diag_ref, dfar_ref,
    table_ref, score_ref, dprob_ref, prob_ref, delta_ref, fold_ref, col_ref, q_two, g_two,
):
    rows = q_ref.shape[0]
    near_len = table_ref.shape[1] - LANES
    keys = jnp.concatenate([k_ref[...], k_label_ref[...]], axis=1)
    weighted = g_ref[...].astype(jnp.float32) * o_ref[...].astype(jnp.float32)
    for head in range(2):
        mask = head_mask(head)
        mask_low = mask.astype(jnp.bfloat16)
        own_q = q_ref[...] * mask_low
        own_g = g_ref[...] * mask_low
        q_two[head * rows : (head + 1) * rows, :] = own_q
        g_two[head * rows : (head + 1) * rows, :] = own_g
        query = jnp.concatenate([own_q, q_label_ref[...]], axis=1)
        score_ref[...] = dot_nt(query, keys)
        dprob_ref[...] = dot_nt(own_g, v_ref[...])
        fill_offsets(base_ref, head, table_ref)
        col_ref[0] = jnp.broadcast_to(
            jnp.sum(weighted * mask, axis=1, keepdims=True), (rows, LANES)
        )
        col_ref[1] = jnp.broadcast_to(
            log_ref[0, :, head * HD : head * HD + 1], (rows, LANES)
        )
        for half in range(rows // LANES):

            def body(step, carry, half=half, head=head):
                row, near, far = score_rows(
                    score_ref, table_ref, far_ref, head, half, step, near_len
                )
                center = col_ref[0, pl.ds(row, GB), 0:1]
                logs = col_ref[1, pl.ds(row, GB), 0:1]
                to_row = pl.multiple_of(head * rows + row, GB)
                near = jnp.exp(near - logs)
                far = jnp.exp(far - logs)
                prob_ref[pl.ds(to_row, GB), :near_len] = near.astype(jnp.bfloat16)
                prob_ref[pl.ds(to_row, GB), near_len:] = far.astype(jnp.bfloat16)
                near = near * (dprob_ref[pl.ds(row, GB), :near_len] - center)
                far = far * (dprob_ref[pl.ds(row, GB), near_len:] - center)
                delta_ref[pl.ds(to_row, GB), :near_len] = near.astype(jnp.bfloat16)
                delta_ref[pl.ds(to_row, GB), near_len:] = far.astype(jnp.bfloat16)
                at = pl.ds(pl.multiple_of(step * GB, GB), GB)
                if half == 0:
                    fold_ref[at, :LANES] = jnp.zeros((GB, LANES), jnp.float32)
                    fold_ref[at, LANES:] = near
                else:
                    fold_ref[at, :near_len] += near
                dfar_ref[0, head, pl.ds(half * (LANES // GB) + step, 1), :] = jnp.sum(
                    far, axis=0, keepdims=True
                )
                return carry

            lax.fori_loop(0, LANES // GB, body, 0, unroll=2)
        diag = fold_ref[0:8, :]
        width = table_ref.shape[1]
        for group in range(1, LANES // 8):
            diag = diag + pltpu.roll(fold_ref[group * 8 : group * 8 + 8, :], width - group * 8, 1)
        diag_ref[0, head] = diag
    low = dot_nn(delta_ref[:rows, :], k_ref[...]) * head_mask(0)
    high = dot_nn(delta_ref[rows:, :], k_ref[...]) * head_mask(1)
    dq_ref[...] = (low + high).astype(jnp.bfloat16)
    dk_ref[...] = dot_tn(q_two[...], delta_ref[...]).T.astype(jnp.bfloat16)
    dv_ref[...] = dot_tn(g_two[...], prob_ref[...]).T.astype(jnp.bfloat16)


def kernel_cost(rows, total):
    return pl.CostEstimate(
        flops=rows * total * PAIRS * LANES * 120, transcendentals=0, bytes_accessed=1 << 20
    )


def attention_specs(rows, total, width, far_len):
    col = lambda p: (0, p)
    return dict(
        q=pl.BlockSpec((rows, LANES), col),
        k=pl.BlockSpec((total, LANES), col),
        q_label=pl.BlockSpec((rows, LANES), lambda p: (0, 0)),
        k_label=pl.BlockSpec((total, LANES), lambda p: (0, 0)),
        base=pl.BlockSpec((1, 2, width), lambda p: (p, 0, 0)),
        far=pl.BlockSpec((1, 2, rows // GB, far_len), lambda p: (p, 0, 0, 0)),
        log=pl.BlockSpec((1, rows, LANES), lambda p: (p, 0, 0)),
        diag=pl.BlockSpec((1, 2, 8, width), lambda p: (p, 0, 0, 0)),
    )


def attention_forward(q, k, v, q_label, k_label, base, far):
    rows, total, width, far_len = q.shape[0], k.shape[0], base.shape[2], far.shape[3]
    s = attention_specs(rows, total, width, far_len)
    return pl.pallas_call(
        forward_kernel,
        grid=(PAIRS,),
        in_specs=[s["q"], s["k"], s["k"], s["q_label"], s["k_label"], s["base"], s["far"]],
        out_specs=[s["q"], s["log"]],
        out_shape=[
            jax.ShapeDtypeStruct((rows, PAIRS * LANES), jnp.bfloat16),
            jax.ShapeDtypeStruct((PAIRS, rows, LANES), jnp.float32),
        ],
        scratch_shapes=[
            pltpu.VMEM((LANES, width), jnp.float32),
            pltpu.VMEM((rows, total), jnp.float32),
            pltpu.VMEM((rows, total), jnp.bfloat16),
            pltpu.VMEM((2, rows, LANES), jnp.float32),
        ],
        compiler_params=pltpu.CompilerParams(vmem_limit_bytes=VMEM_LIMIT),
        cost_estimate=kernel_cost(rows, total),
        name="attention_forward",
    )(q, k, v, q_label, k_label, base, far)


def attention_backward(q, k, v, g, o, logs, q_label, k_label, base, far):
    rows, total, width, far_len = q.shape[0], k.shape[0], base.shape[2], far.shape[3]
    s = attention_specs(rows, total, width, far_len)
    return pl.pallas_call(
        backward_kernel,
        grid=(PAIRS,),
        in_specs=[
            s["q"], s["k"], s["k"], s["q"], s["q"], s["log"],
            s["q_label"], s["k_label"], s["base"], s["far"],
        ],
        out_specs=[s["q"], s["k"], s["k"], s["diag"], s["far"]],
        out_shape=[
            jax.ShapeDtypeStruct((rows, PAIRS * LANES), jnp.bfloat16),
            jax.ShapeDtypeStruct((total, PAIRS * LANES), jnp.bfloat16),
            jax.ShapeDtypeStruct((total, PAIRS * LANES), jnp.bfloat16),
            jax.ShapeDtypeStruct((PAIRS, 2, 8, width), jnp.float32),
            jax.ShapeDtypeStruct((PAIRS, 2, rows // GB, far_len), jnp.float32),
        ],
        scratch_shapes=[
            pltpu.VMEM((LANES, width), jnp.float32),
            pltpu.VMEM((rows, total), jnp.float32),
            pltpu.VMEM((rows, total), jnp.float32),
            pltpu.VMEM((2 * rows, total), jnp.bfloat16),
            pltpu.VMEM((2 * rows, total), jnp.bfloat16),
            pltpu.VMEM((LANES, width), jnp.float32),
            pltpu.VMEM((2, rows, LANES), jnp.float32),
            pltpu.VMEM((2 * rows, LANES), jnp.bfloat16),
            pltpu.VMEM((2 * rows, LANES), jnp.bfloat16),
        ],
        compiler_params=pltpu.CompilerParams(vmem_limit_bytes=VMEM_LIMIT),
        cost_estimate=kernel_cost(rows, total),
        name="attention_backward",
    )(q, k, v, g, o, logs, q_label, k_label, base, far)


def on_device(
    hidden, cotangent, query_proj, key_proj, value_proj, out_proj, gate_proj, up_proj,
    down_proj, first_gain, second_gain, global_gain, local_bias, side_bias,
    segments, local_buckets, global_buckets,
):
    x_own = hidden[0]
    cot = cotangent[0]
    rows, width = x_own.shape
    cycle_size = lax.axis_size(CTX)
    cycle_index = lax.axis_index(CTX)
    first_row = cycle_index * rows
    far_len = rows * cycle_size // GB
    own_blocks = rows // GB
    reach = HALF // rows
    near_len = rows + 2 * HALF

    left = [shifted(x_own, CTX, d) for d in range(reach, 0, -1)]
    right = [shifted(x_own, CTX, -d) for d in range(1, reach + 1)]
    window = jnp.concatenate(left + [x_own] + right, axis=0)

    gather = lambda a: lax.all_gather(a, SHARD, axis=0, tiled=True)
    whole = lambda a: a.reshape(-1, a.shape[-1])
    first_set = gather(jnp.stack([query_proj, key_proj, value_proj, out_proj])[None])
    first_set, down_part = fence(first_set, pick(halves(down_proj), lax.axis_index("y")))
    from_x = swapped(down_part, "x")
    w_query, w_key, w_value, w_out = [whole(first_set[:, i]) for i in range(4)]
    second_set = gather(jnp.stack([gate_proj, up_proj])[None])
    w_gate, w_up = [whole(second_set[:, i]) for i in range(2)]
    small = jnp.concatenate(
        [first_gain, second_gain, global_gain, local_bias.reshape(-1), side_bias.reshape(-1)]
    )
    small = gather(small[None])
    cut = first_gain.shape[0]
    gain_one = small[:, :cut].reshape(-1).astype(jnp.float32)
    gain_two = small[:, cut : 2 * cut].reshape(-1).astype(jnp.float32)
    gain_side = small[:, 2 * cut : 3 * cut].reshape(-1).astype(jnp.float32)
    tab = local_bias.size
    near_tab = small[:, 3 * cut : 3 * cut + tab].reshape(NB, H)
    side_tab = small[:, 3 * cut + tab :].reshape(NB, H)

    bucket_iota = jnp.arange(NB, dtype=jnp.int32)[None, :]
    onehot_near = (local_buckets[:, None] == bucket_iota).astype(jnp.bfloat16)
    near_row = lax.dot_general(
        near_tab, onehot_near, (((0,), (1,)), ((), ())), preferred_element_type=jnp.float32
    )
    table_width = near_len + LANES
    base = jnp.pad(
        near_row,
        ((0, 0), (LANES + 1, table_width - LANES - 1 - near_row.shape[1])),
        constant_values=NEG,
    ).reshape(PAIRS, 2, table_width)
    far_start = far_len - own_blocks - cycle_index * own_blocks
    bucket_slice = lax.dynamic_slice_in_dim(global_buckets, far_start, far_len + own_blocks - 1, 0)
    onehot_side = (bucket_slice[:, None] == bucket_iota).astype(jnp.bfloat16)
    side_row = lax.dot_general(
        side_tab, onehot_side, (((0,), (1,)), ((), ())), preferred_element_type=jnp.float32
    )
    far = jnp.stack(
        [side_row[:, own_blocks - 1 - r : own_blocks - 1 - r + far_len] for r in range(own_blocks)],
        axis=1,
    ).reshape(PAIRS, 2, own_blocks, far_len)
    labels = segments[0]
    label_iota = jnp.arange(LANES, dtype=jnp.int32)[None, :]
    label_query = lax.dynamic_slice_in_dim(labels, first_row, rows, 0)
    label_pad = jnp.pad(labels, (HALF, HALF), constant_values=-1)
    label_window = lax.dynamic_slice_in_dim(label_pad, first_row, near_len, 0)
    label_keys = jnp.concatenate([label_window, labels[::GB]])
    q_label = (label_query[:, None] == label_iota).astype(jnp.bfloat16)
    k_label = jnp.where(label_keys[:, None] == label_iota, 0.0, NEG).astype(jnp.bfloat16)

    wide = window.astype(jnp.float32)
    scale_wide = rms_scale(wide)
    normed_wide = ((wide * scale_wide) * gain_one).astype(jnp.bfloat16)
    inputs = x_own.astype(jnp.float32)
    scale_one = rms_scale(inputs)
    normed_one = inputs * scale_one
    normed = (normed_one * gain_one).astype(jnp.bfloat16)
    block_sums = jnp.sum(normed.astype(jnp.float32).reshape(own_blocks, GB, width), axis=1)
    scale_side = rms_scale(block_sums)
    normed_side = block_sums * scale_side
    side_rows = (normed_side * gain_side).astype(jnp.bfloat16)
    all_rows = gather_over(gather_over(side_rows, "y", [1]), "z", bits("z"))
    key_rows = jnp.concatenate([normed_wide, all_rows], axis=0)
    queries = dot_nn(normed, w_query).astype(jnp.bfloat16)
    keys = dot_nn(key_rows, w_key).astype(jnp.bfloat16)
    values = dot_nn(key_rows, w_value).astype(jnp.bfloat16)
    queries, keys, values = fence(queries, keys, values)
    attended, logs = attention_forward(queries, keys, values, q_label, k_label, base, far)
    attended, logs, from_x = fence(attended, logs, from_x)
    from_y = swapped(from_x, "y")
    middle = inputs + dot_nn(attended, w_out)
    scale_two = rms_scale(middle)
    normed_two = middle * scale_two
    ffn_in = (normed_two * gain_two).astype(jnp.bfloat16)
    ffn_in, from_y = fence(ffn_in, from_y)
    pair = in_order(from_x, from_y, lax.axis_index("y"))
    pair = in_order(down_proj[None], pair[None], lax.axis_index("x"))
    other = swapped(pair, "c")
    gate_pre = dot_nn(ffn_in, w_gate)
    up_pre = dot_nn(ffn_in, w_up)
    gate_pre, up_pre, other = fence(gate_pre, up_pre, other)
    w_down = whole(in_order(pair[:, None], other[:, None], lax.axis_index("c"), 1))
    gelu_out, gelu_pull = jax.vjp(lambda v: jax.nn.gelu(v, approximate=True), gate_pre)
    product = (gelu_out * up_pre).astype(jnp.bfloat16)
    outputs = (middle + dot_nn(product, w_down)).astype(jnp.bfloat16)

    down_grad = dot_tn(product, cot)
    product_grad = dot_nt(cot, w_down)
    gate_delta = gelu_pull(product_grad * up_pre)[0].astype(jnp.bfloat16)
    up_delta = (product_grad * gelu_out).astype(jnp.bfloat16)
    gate_grad = dot_tn(ffn_in, gate_delta)
    up_grad = dot_tn(ffn_in, up_delta)
    ffn_back = dot_nt(gate_delta, w_gate) + dot_nt(up_delta, w_up)
    second_part = jnp.sum(ffn_back * normed_two, axis=0)
    middle_grad = cot.astype(jnp.float32) + norm_back(ffn_back, normed_two, scale_two, gain_two)
    mixed_grad = middle_grad.astype(jnp.bfloat16)
    out_grad = dot_tn(attended, mixed_grad)
    attended_grad = dot_nt(mixed_grad, w_out).astype(jnp.bfloat16)

    cut, deep = query_proj.shape[0], down_proj.shape[0]
    plane = lambda a: lax.psum_scatter(a, ("x", "y"), scatter_dimension=0, tiled=True)
    down_sum = jnp.concatenate(core_sums([down_grad, out_grad], [deep, cut]), axis=1)
    pair = core_sums([gate_grad, up_grad], [cut] * 2)
    attended_grad, down_sum, pair = fence(attended_grad, whole(down_sum), pair)
    down_sum = plane(down_sum)
    pair = pair_first(*pair)

    dq, dk, dv, diag, dfar = attention_backward(
        queries, keys, values, attended_grad, attended, logs, q_label, k_label, base, far
    )
    up_z, down_z = bits("z"), bits("z")[::-1]
    near_z, rest_z = up_z[:1], up_z[1:]

    dq, dk, dv, diag, dfar, pair = fence(dq, dk, dv, diag, dfar, pair)
    pair = pair_second(*pair)
    far_back = dot_nt(dk[near_len:], w_key) + dot_nt(dv[near_len:], w_value)
    side_back = scatter_over(far_back.astype(jnp.bfloat16), "z", down_z[:-1])
    query_grad = dot_tn(normed, dq).astype(jnp.bfloat16)
    key_grad = dot_tn(key_rows, dk).astype(jnp.bfloat16)
    value_grad = dot_tn(key_rows, dv).astype(jnp.bfloat16)

    dq, dk, dv, query_grad, key_grad, value_grad, side_back, pair = fence(
        dq, dk, dv, query_grad, key_grad, value_grad, side_back, pair
    )
    three = jnp.concatenate(core_sums([query_grad, key_grad, value_grad], [cut] * 3), axis=1)
    pair = scatter_over(pair, "z", near_z)
    side_back = scatter_over(side_back, "z", down_z[-1:])
    key_back = dot_nt(dk[:near_len], w_key) + dot_nt(dv[:near_len], w_value)
    own_start = reach * rows
    normed_back = dot_nt(dq, w_query) + key_back[own_start : own_start + rows]
    back_low = key_back.astype(jnp.bfloat16)

    three, normed_back, back_low, side_back, pair, down_sum = fence(
        whole(three), normed_back, back_low, side_back, pair, down_sum
    )
    down_sum = scatter_over(down_sum, "z", near_z)
    three = scatter_over(three, "x", bits("x"))
    pair = scatter_over(pair, "z", rest_z)
    side_back = scatter_over(side_back, "y", [1]).astype(jnp.float32)
    low_y = lax.axis_index("y") == 0
    blocks = back_low.reshape(2 * reach + 1, rows, width)
    near_by = jnp.where(low_y, blocks[3], blocks[1])
    farther = jnp.where(low_y, blocks[1], blocks[3])
    got = swapped(jnp.stack([near_by, farther]), "y")

    three, got, side_back, normed_back, blocks, pair, down_sum = fence(
        three, got, side_back, normed_back, blocks, pair, down_sum
    )
    down_sum = scatter_over(down_sum, "z", rest_z)
    three = scatter_over(three, "y", [1])
    pair = gather_over(pair, "z", rest_z[::-1])
    zero = jnp.zeros_like(got[1])
    upward = shifted(add_low(blocks[4], jnp.where(low_y, got[1], zero)), "z", 1)
    downward = shifted(add_low(blocks[0], jnp.where(low_y, zero, got[1])), "z", -1)
    got = [got[0], upward, downward]
    global_part = jnp.sum(side_back * normed_side, axis=0)
    sums_grad = norm_back(side_back, normed_side, scale_side, gain_side)
    normed_back = (
        normed_back.reshape(own_blocks, GB, width) + sums_grad[:, None, :]
    ).reshape(rows, width)

    diag = diag.reshape(H, 8, table_width)
    near_sum = diag[:, 0]
    for r in range(1, 8):
        near_sum = near_sum + jnp.roll(diag[:, r], -r, axis=1)
    near_sum = near_sum[:, LANES + 1 : LANES + 2 * HALF]
    local_part = lax.dot_general(
        near_sum, onehot_near.astype(jnp.float32), (((1,), (0,)), ((), ())), precision=HIGHEST
    )
    dfar = dfar.reshape(H, own_blocks, far_len)
    side_sum = sum(
        jnp.pad(dfar[:, r], ((0, 0), (own_blocks - 1 - r, r))) for r in range(own_blocks)
    )
    side_part = lax.dot_general(
        side_sum, onehot_side.astype(jnp.float32), (((1,), (0,)), ((), ())), precision=HIGHEST
    )

    three, normed_back, got, local_part, side_part, global_part, pair, down_sum = fence(
        three, normed_back, got, local_part, side_part, global_part, pair, down_sum
    )
    three = scatter_over(three, "z", near_z)
    pair = gather_over(pair, "z", near_z)
    down_sum = gather_over(down_sum, "z", rest_z[::-1])
    for piece in got:
        normed_back = normed_back + piece.astype(jnp.float32)
    first_part = jnp.sum(normed_back * normed_one, axis=0)
    hidden_grad = (
        middle_grad + norm_back(normed_back, normed_one, scale_one, gain_one)
    ).astype(jnp.bfloat16)
    tables = jnp.concatenate([local_part, side_part], axis=0)
    tiny = jnp.concatenate(
        [
            jnp.stack([first_part, second_part, global_part]),
            jnp.pad(tables, ((0, 5), (0, width - tables.shape[1]))),
        ]
    )

    three = scatter_over(three, "z", rest_z)
    pair = gather_over(pair, "y", [1])
    down_sum = gather_over(down_sum, "z", near_z)
    tiny = tiny + swapped(tiny, "c")
    tiny = tiny + swapped(tiny, "x")

    three, tiny, pair, down_sum = fence(three, tiny, pair, down_sum)
    three = gather_over(three, "z", rest_z[::-1])
    down_sum = gather_over(down_sum, "y", [1])
    tiny = tiny + swapped(tiny, "y")

    three = gather_over(three, "z", near_z)
    for bit in near_z:
        tiny = tiny + swapped(tiny, "z", bit)

    three, tiny = fence(three, tiny)
    three = gather_over(three, "y", [1]).reshape(3, cut, -1)
    for bit in rest_z:
        tiny = tiny + swapped(tiny, "z", bit)
    pair = pair.reshape(2, 2, cut // 2, -1)
    pair = pair[:, 0].reshape(cut, -1), pair[:, 1].reshape(cut, -1)
    big = [three[0], three[1], three[2], down_sum[deep:], pair[0], pair[1], down_sum[:deep]]
    big = [a.astype(jnp.float32) for a in big]
    shards = lax.axis_size(SHARD)
    shard = lax.axis_index(SHARD)
    own = lax.dynamic_slice_in_dim(tiny[:3], shard * cut, cut, 1)
    bias_rows = NB // shards
    own_tables = lax.dynamic_slice_in_dim(tiny[3 : 3 + 2 * H, :NB], shard * bias_rows, bias_rows, 1).T
    done = [own[0], own[1], own[2], own_tables[:, :H], own_tables[:, H:]]
    return (outputs[None], hidden_grad[None], *big, *done)


def solution(mesh):
    ctx, shard = mesh.shape["ctx"], mesh.shape["shard"]
    fine = jax.sharding.Mesh(
        mesh.devices.reshape(ctx // 2, 2, shard // 2, 2), CTX + SHARD
    )
    tokens = P(SHARD, CTX, None)
    weight = P(SHARD, None)
    gain = P(SHARD)
    return jax.shard_map(
        on_device,
        mesh=fine,
        in_specs=(tokens, tokens) + (weight,) * 7 + (gain,) * 3 + (weight,) * 3 + (P(), P()),
        out_specs=(tokens, tokens) + (weight,) * 7 + (gain,) * 3 + (weight,) * 2,
        check_vma=False,
    )
```

```python
import jax
import jax.numpy as jnp
from jax import lax
from jax.experimental import pallas as pl
from jax.experimental.pallas import tpu as pltpu
from jax.sharding import PartitionSpec as P

H = 12
HD = 64
NB = 32
GB = 16
HALF = 512
LANES = 128
PAIRS = H * HD // LANES

EPS = 1e-06
NEG = -1e30
HIGHEST = lax.Precision.HIGHEST


CTX = ("z", "y")
SHARD = ("x", "c")


def shifted(value, axis, by):
    length = lax.axis_size(axis)
    pairs = [(i, i + by) for i in range(length) if 0 <= i + by < length]
    return lax.ppermute(value, axis, pairs)


def swapped(value, axis, bit=1):
    return lax.ppermute(value, axis, [(i, i ^ bit) for i in range(lax.axis_size(axis))])


def pick(value, index, dim=0):
    return lax.dynamic_index_in_dim(value, index, dim, keepdims=False)


def bit_of(axis, bit):
    return (lax.axis_index(axis) // bit) % 2


def halves(value):
    return value.reshape(2, value.shape[0] // 2, *value.shape[1:])


def in_order(own, other, upper, dim=0):
    return jnp.where(
        upper == 1,
        jnp.concatenate([other, own], axis=dim),
        jnp.concatenate([own, other], axis=dim),
    )


def add_low(left, right):
    return (left.astype(jnp.float32) + right.astype(jnp.float32)).astype(jnp.bfloat16)


def bits(axis):
    return [1 << k for k in range(lax.axis_size(axis).bit_length() - 1)]


def scatter_over(value, axis, order):
    for bit in order:
        both, mine = halves(value), bit_of(axis, bit)
        value = add_low(pick(both, mine), swapped(pick(both, 1 - mine), axis, bit))
    return value


def gather_over(value, axis, order):
    for bit in order:
        value = in_order(value, swapped(value, axis, bit), bit_of(axis, bit))
    return value


def fence(*values):
    return lax.optimization_barrier(values)


def core_sums(grads, rows):
    core = lax.axis_index("c")
    split = [a.astype(jnp.bfloat16).reshape(2, 2, r, a.shape[1]) for a, r in zip(grads, rows)]
    got = [swapped(pick(a, 1 - core, 1), "c") for a in split]
    return [add_low(pick(a, core, 1), b) for a, b in zip(split, got)]


def pair_first(one, two):
    x, y = lax.axis_index("x"), lax.axis_index("y")
    two = two.reshape(2, 2, two.shape[1] // 2, two.shape[2])
    got_one = swapped(pick(one, 1 - x), "x")
    got_two = swapped(pick(two, 1 - y, 1), "y")
    return add_low(pick(one, x), got_one), add_low(pick(two, y, 1), got_two)


def pair_second(one, two):
    x, y = lax.axis_index("x"), lax.axis_index("y")
    one = halves(one)
    got_one = swapped(pick(one, 1 - y), "y")
    got_two = swapped(pick(two, 1 - x), "x")
    one = add_low(pick(one, y), got_one)
    two = add_low(pick(two, x), got_two)
    return jnp.concatenate([one, two], axis=0)


def dot_nn(left, right):
    return lax.dot_general(
        left, right, (((1,), (0,)), ((), ())), preferred_element_type=jnp.float32
    )


def dot_nt(left, right):
    return lax.dot_general(
        left, right, (((1,), (1,)), ((), ())), preferred_element_type=jnp.float32
    )


def dot_tn(left, right):
    return lax.dot_general(
        left, right, (((0,), (0,)), ((), ())), preferred_element_type=jnp.float32
    )


def rms_scale(values):
    return lax.rsqrt(jnp.mean(values * values, axis=-1, keepdims=True) + EPS)


def norm_back(upstream, normed_val, row_scale, gain_row):
    scaled = upstream * gain_row
    return row_scale * (scaled - normed_val * jnp.mean(scaled * normed_val, axis=-1, keepdims=True))


def head_mask(head):
    lane = lax.broadcasted_iota(jnp.int32, (1, LANES), 1)
    own = (lane < HD) if head == 0 else (lane >= HD)
    return own.astype(jnp.float32)


def fill_offsets(base_ref, head, table_ref):
    width = table_ref.shape[1]
    base = jnp.broadcast_to(base_ref[0, head : head + 1, :], (8, width))
    base = pltpu.roll(base, 0, 1, stride=1, stride_axis=0)
    for group in range(LANES // 8):
        table_ref[group * 8 : group * 8 + 8, :] = (
            pltpu.roll(base, group * 8, 1) if group else base
        )


def score_rows(score_ref, table_ref, far_ref, head, half, step, near_len):
    row = pl.multiple_of(half * LANES + step * GB, GB)
    start = LANES if half == 0 else 0
    bias = table_ref[pl.ds(pl.multiple_of(step * GB, GB), GB), start : start + near_len]
    near = score_ref[pl.ds(row, GB), :near_len] + bias
    far = score_ref[pl.ds(row, GB), near_len:] + far_ref[
        0, head, pl.ds(half * (LANES // GB) + step, 1), :
    ]
    return row, near, far


def forward_kernel(
    q_ref, k_ref, v_ref, q_label_ref, k_label_ref, base_ref, far_ref,
    out_ref, log_ref,
    table_ref, score_ref, prob_ref, total_ref,
):
    rows = q_ref.shape[0]
    near_len = table_ref.shape[1] - LANES
    keys = jnp.concatenate([k_ref[...], k_label_ref[...]], axis=1)
    out = None
    logs = None
    for head in range(2):
        mask = head_mask(head)
        query = jnp.concatenate(
            [q_ref[...] * mask.astype(jnp.bfloat16), q_label_ref[...]], axis=1
        )
        score_ref[...] = dot_nt(query, keys)
        fill_offsets(base_ref, head, table_ref)
        for half in range(rows // LANES):

            def body(step, carry, half=half, head=head):
                row, near, far = score_rows(
                    score_ref, table_ref, far_ref, head, half, step, near_len
                )
                peak = jnp.maximum(
                    jnp.max(near, axis=1, keepdims=True), jnp.max(far, axis=1, keepdims=True)
                )
                near = jnp.exp(near - peak)
                far = jnp.exp(far - peak)
                total = jnp.sum(near, axis=1, keepdims=True) + jnp.sum(far, axis=1, keepdims=True)
                prob_ref[pl.ds(row, GB), :near_len] = near.astype(jnp.bfloat16)
                prob_ref[pl.ds(row, GB), near_len:] = far.astype(jnp.bfloat16)
                total_ref[0, pl.ds(row, GB), :] = jnp.broadcast_to(total, (GB, LANES))
                total_ref[1, pl.ds(row, GB), :] = jnp.broadcast_to(
                    peak + jnp.log(total), (GB, LANES)
                )
                return carry

            lax.fori_loop(0, LANES // GB, body, 0, unroll=2)
        mixed = dot_nn(prob_ref[...], v_ref[...]) / total_ref[0] * mask
        out = mixed if out is None else out + mixed
        part = total_ref[1] * mask
        logs = part if logs is None else logs + part
    out_ref[...] = out.astype(jnp.bfloat16)
    log_ref[0] = logs


def backward_kernel(
    q_ref, k_ref, v_ref, g_ref, o_ref, log_ref, q_label_ref, k_label_ref, base_ref, far_ref,
    dq_ref, dk_ref, dv_ref, diag_ref, dfar_ref,
    table_ref, score_ref, dprob_ref, prob_ref, delta_ref, fold_ref, col_ref, q_two, g_two,
):
    rows = q_ref.shape[0]
    near_len = table_ref.shape[1] - LANES
    keys = jnp.concatenate([k_ref[...], k_label_ref[...]], axis=1)
    weighted = g_ref[...].astype(jnp.float32) * o_ref[...].astype(jnp.float32)
    for head in range(2):
        mask = head_mask(head)
        mask_low = mask.astype(jnp.bfloat16)
        own_q = q_ref[...] * mask_low
        own_g = g_ref[...] * mask_low
        q_two[head * rows : (head + 1) * rows, :] = own_q
        g_two[head * rows : (head + 1) * rows, :] = own_g
        query = jnp.concatenate([own_q, q_label_ref[...]], axis=1)
        score_ref[...] = dot_nt(query, keys)
        dprob_ref[...] = dot_nt(own_g, v_ref[...])
        fill_offsets(base_ref, head, table_ref)
        col_ref[0] = jnp.broadcast_to(
            jnp.sum(weighted * mask, axis=1, keepdims=True), (rows, LANES)
        )
        col_ref[1] = jnp.broadcast_to(
            log_ref[0, :, head * HD : head * HD + 1], (rows, LANES)
        )
        for half in range(rows // LANES):

            def body(step, carry, half=half, head=head):
                row, near, far = score_rows(
                    score_ref, table_ref, far_ref, head, half, step, near_len
                )
                center = col_ref[0, pl.ds(row, GB), 0:1]
                logs = col_ref[1, pl.ds(row, GB), 0:1]
                to_row = pl.multiple_of(head * rows + row, GB)
                near = jnp.exp(near - logs)
                far = jnp.exp(far - logs)
                prob_ref[pl.ds(to_row, GB), :near_len] = near.astype(jnp.bfloat16)
                prob_ref[pl.ds(to_row, GB), near_len:] = far.astype(jnp.bfloat16)
                near = near * (dprob_ref[pl.ds(row, GB), :near_len] - center)
                far = far * (dprob_ref[pl.ds(row, GB), near_len:] - center)
                delta_ref[pl.ds(to_row, GB), :near_len] = near.astype(jnp.bfloat16)
                delta_ref[pl.ds(to_row, GB), near_len:] = far.astype(jnp.bfloat16)
                at = pl.ds(pl.multiple_of(step * GB, GB), GB)
                if half == 0:
                    fold_ref[at, :LANES] = jnp.zeros((GB, LANES), jnp.float32)
                    fold_ref[at, LANES:] = near
                else:
                    fold_ref[at, :near_len] += near
                dfar_ref[0, head, pl.ds(half * (LANES // GB) + step, 1), :] = jnp.sum(
                    far, axis=0, keepdims=True
                )
                return carry

            lax.fori_loop(0, LANES // GB, body, 0, unroll=2)
        diag = fold_ref[0:8, :]
        width = table_ref.shape[1]
        for group in range(1, LANES // 8):
            diag = diag + pltpu.roll(fold_ref[group * 8 : group * 8 + 8, :], width - group * 8, 1)
        diag_ref[0, head] = diag
    low = dot_nn(delta_ref[:rows, :], k_ref[...]) * head_mask(0)
    high = dot_nn(delta_ref[rows:, :], k_ref[...]) * head_mask(1)
    dq_ref[...] = (low + high).astype(jnp.bfloat16)
    dk_ref[...] = dot_tn(q_two[...], delta_ref[...]).T.astype(jnp.bfloat16)
    dv_ref[...] = dot_tn(g_two[...], prob_ref[...]).T.astype(jnp.bfloat16)


def kernel_cost(rows, total):
    return pl.CostEstimate(
        flops=rows * total * PAIRS * LANES * 120, transcendentals=0, bytes_accessed=1 << 20
    )


def attention_specs(rows, total, width, far_len):
    col = lambda p: (0, p)
    return dict(
        q=pl.BlockSpec((rows, LANES), col),
        k=pl.BlockSpec((total, LANES), col),
        q_label=pl.BlockSpec((rows, LANES), lambda p: (0, 0)),
        k_label=pl.BlockSpec((total, LANES), lambda p: (0, 0)),
        base=pl.BlockSpec((1, 2, width), lambda p: (p, 0, 0)),
        far=pl.BlockSpec((1, 2, rows // GB, far_len), lambda p: (p, 0, 0, 0)),
        log=pl.BlockSpec((1, rows, LANES), lambda p: (p, 0, 0)),
        diag=pl.BlockSpec((1, 2, 8, width), lambda p: (p, 0, 0, 0)),
    )


def attention_forward(q, k, v, q_label, k_label, base, far):
    rows, total, width, far_len = q.shape[0], k.shape[0], base.shape[2], far.shape[3]
    s = attention_specs(rows, total, width, far_len)
    return pl.pallas_call(
        forward_kernel,
        grid=(PAIRS,),
        in_specs=[s["q"], s["k"], s["k"], s["q_label"], s["k_label"], s["base"], s["far"]],
        out_specs=[s["q"], s["log"]],
        out_shape=[
            jax.ShapeDtypeStruct((rows, PAIRS * LANES), jnp.bfloat16),
            jax.ShapeDtypeStruct((PAIRS, rows, LANES), jnp.float32),
        ],
        scratch_shapes=[
            pltpu.VMEM((LANES, width), jnp.float32),
            pltpu.VMEM((rows, total), jnp.float32),
            pltpu.VMEM((rows, total), jnp.bfloat16),
            pltpu.VMEM((2, rows, LANES), jnp.float32),
        ],
        compiler_params=pltpu.CompilerParams(vmem_limit_bytes=rows * total * 36),
        cost_estimate=kernel_cost(rows, total),
        name="attention_forward",
    )(q, k, v, q_label, k_label, base, far)


def attention_backward(q, k, v, g, o, logs, q_label, k_label, base, far):
    rows, total, width, far_len = q.shape[0], k.shape[0], base.shape[2], far.shape[3]
    s = attention_specs(rows, total, width, far_len)
    return pl.pallas_call(
        backward_kernel,
        grid=(PAIRS,),
        in_specs=[
            s["q"], s["k"], s["k"], s["q"], s["q"], s["log"],
            s["q_label"], s["k_label"], s["base"], s["far"],
        ],
        out_specs=[s["q"], s["k"], s["k"], s["diag"], s["far"]],
        out_shape=[
            jax.ShapeDtypeStruct((rows, PAIRS * LANES), jnp.bfloat16),
            jax.ShapeDtypeStruct((total, PAIRS * LANES), jnp.bfloat16),
            jax.ShapeDtypeStruct((total, PAIRS * LANES), jnp.bfloat16),
            jax.ShapeDtypeStruct((PAIRS, 2, 8, width), jnp.float32),
            jax.ShapeDtypeStruct((PAIRS, 2, rows // GB, far_len), jnp.float32),
        ],
        scratch_shapes=[
            pltpu.VMEM((LANES, width), jnp.float32),
            pltpu.VMEM((rows, total), jnp.float32),
            pltpu.VMEM((rows, total), jnp.float32),
            pltpu.VMEM((2 * rows, total), jnp.bfloat16),
            pltpu.VMEM((2 * rows, total), jnp.bfloat16),
            pltpu.VMEM((LANES, width), jnp.float32),
            pltpu.VMEM((2, rows, LANES), jnp.float32),
            pltpu.VMEM((2 * rows, LANES), jnp.bfloat16),
            pltpu.VMEM((2 * rows, LANES), jnp.bfloat16),
        ],
        compiler_params=pltpu.CompilerParams(vmem_limit_bytes=rows * total * 36),
        cost_estimate=kernel_cost(rows, total),
        name="attention_backward",
    )(q, k, v, g, o, logs, q_label, k_label, base, far)


def on_device(
    hidden, cotangent, query_proj, key_proj, value_proj, out_proj, gate_proj, up_proj,
    down_proj, first_gain, second_gain, global_gain, local_bias, side_bias,
    segments, local_buckets, global_buckets,
):
    x_own = hidden[0]
    cot = cotangent[0]
    rows, width = x_own.shape
    cycle_size = lax.axis_size(CTX)
    cycle_index = lax.axis_index(CTX)
    first_row = cycle_index * rows
    far_len = rows * cycle_size // GB
    own_blocks = rows // GB
    reach = HALF // rows
    near_len = rows + 2 * HALF

    left = [shifted(x_own, CTX, d) for d in range(reach, 0, -1)]
    right = [shifted(x_own, CTX, -d) for d in range(1, reach + 1)]
    window = jnp.concatenate(left + [x_own] + right, axis=0)

    gather = lambda a: lax.all_gather(a, SHARD, axis=0, tiled=True)
    whole = lambda a: a.reshape(-1, a.shape[-1])
    first_set = gather(jnp.stack([query_proj, key_proj, value_proj, out_proj])[None])
    first_set, down_part = fence(first_set, pick(halves(down_proj), lax.axis_index("y")))
    from_x = swapped(down_part, "x")
    w_query, w_key, w_value, w_out = [whole(first_set[:, i]) for i in range(4)]
    second_set = gather(jnp.stack([gate_proj, up_proj])[None])
    w_gate, w_up = [whole(second_set[:, i]) for i in range(2)]
    small = jnp.concatenate(
        [first_gain, second_gain, global_gain, local_bias.reshape(-1), side_bias.reshape(-1)]
    )
    small = gather(small[None])
    cut = first_gain.shape[0]
    gain_one = small[:, :cut].reshape(-1).astype(jnp.float32)
    gain_two = small[:, cut : 2 * cut].reshape(-1).astype(jnp.float32)
    gain_side = small[:, 2 * cut : 3 * cut].reshape(-1).astype(jnp.float32)
    tab = local_bias.size
    near_tab = small[:, 3 * cut : 3 * cut + tab].reshape(NB, H)
    side_tab = small[:, 3 * cut + tab :].reshape(NB, H)

    bucket_iota = jnp.arange(NB, dtype=jnp.int32)[None, :]
    onehot_near = (local_buckets[:, None] == bucket_iota).astype(jnp.bfloat16)
    near_row = lax.dot_general(
        near_tab, onehot_near, (((0,), (1,)), ((), ())), preferred_element_type=jnp.float32
    )
    table_width = near_len + LANES
    base = jnp.pad(
        near_row,
        ((0, 0), (LANES + 1, table_width - LANES - 1 - near_row.shape[1])),
        constant_values=NEG,
    ).reshape(PAIRS, 2, table_width)
    far_start = far_len - own_blocks - cycle_index * own_blocks
    bucket_slice = lax.dynamic_slice_in_dim(global_buckets, far_start, far_len + own_blocks - 1, 0)
    onehot_side = (bucket_slice[:, None] == bucket_iota).astype(jnp.bfloat16)
    side_row = lax.dot_general(
        side_tab, onehot_side, (((0,), (1,)), ((), ())), preferred_element_type=jnp.float32
    )
    far = jnp.stack(
        [side_row[:, own_blocks - 1 - r : own_blocks - 1 - r + far_len] for r in range(own_blocks)],
        axis=1,
    ).reshape(PAIRS, 2, own_blocks, far_len)
    labels = segments[0]
    label_iota = jnp.arange(LANES, dtype=jnp.int32)[None, :]
    label_query = lax.dynamic_slice_in_dim(labels, first_row, rows, 0)
    label_pad = jnp.pad(labels, (HALF, HALF), constant_values=-1)
    label_window = lax.dynamic_slice_in_dim(label_pad, first_row, near_len, 0)
    label_keys = jnp.concatenate([label_window, labels[::GB]])
    q_label = (label_query[:, None] == label_iota).astype(jnp.bfloat16)
    k_label = jnp.where(label_keys[:, None] == label_iota, 0.0, NEG).astype(jnp.bfloat16)

    wide = window.astype(jnp.float32)
    scale_wide = rms_scale(wide)
    normed_wide = ((wide * scale_wide) * gain_one).astype(jnp.bfloat16)
    inputs = x_own.astype(jnp.float32)
    scale_one = rms_scale(inputs)
    normed_one = inputs * scale_one
    normed = (normed_one * gain_one).astype(jnp.bfloat16)
    block_sums = jnp.sum(normed.astype(jnp.float32).reshape(own_blocks, GB, width), axis=1)
    scale_side = rms_scale(block_sums)
    normed_side = block_sums * scale_side
    side_rows = (normed_side * gain_side).astype(jnp.bfloat16)
    all_rows = gather_over(gather_over(side_rows, "y", [1]), "z", bits("z"))
    key_rows = jnp.concatenate([normed_wide, all_rows], axis=0)
    queries = dot_nn(normed, w_query).astype(jnp.bfloat16)
    keys = dot_nn(key_rows, w_key).astype(jnp.bfloat16)
    values = dot_nn(key_rows, w_value).astype(jnp.bfloat16)
    queries, keys, values = fence(queries, keys, values)
    attended, logs = attention_forward(queries, keys, values, q_label, k_label, base, far)
    attended, logs, from_x = fence(attended, logs, from_x)
    from_y = swapped(from_x, "y")
    middle = inputs + dot_nn(attended, w_out)
    scale_two = rms_scale(middle)
    normed_two = middle * scale_two
    ffn_in = (normed_two * gain_two).astype(jnp.bfloat16)
    ffn_in, from_y = fence(ffn_in, from_y)
    pair = in_order(from_x, from_y, lax.axis_index("y"))
    pair = in_order(down_proj[None], pair[None], lax.axis_index("x"))
    other = swapped(pair, "c")
    gate_pre = dot_nn(ffn_in, w_gate)
    up_pre = dot_nn(ffn_in, w_up)
    gate_pre, up_pre, other = fence(gate_pre, up_pre, other)
    w_down = whole(in_order(pair[:, None], other[:, None], lax.axis_index("c"), 1))
    gelu_out, gelu_pull = jax.vjp(lambda v: jax.nn.gelu(v, approximate=True), gate_pre)
    product = (gelu_out * up_pre).astype(jnp.bfloat16)
    outputs = (middle + dot_nn(product, w_down)).astype(jnp.bfloat16)

    down_grad = dot_tn(product, cot)
    product_grad = dot_nt(cot, w_down)
    gate_delta = gelu_pull(product_grad * up_pre)[0].astype(jnp.bfloat16)
    up_delta = (product_grad * gelu_out).astype(jnp.bfloat16)
    gate_grad = dot_tn(ffn_in, gate_delta)
    up_grad = dot_tn(ffn_in, up_delta)
    ffn_back = dot_nt(gate_delta, w_gate) + dot_nt(up_delta, w_up)
    second_part = jnp.sum(ffn_back * normed_two, axis=0)
    middle_grad = cot.astype(jnp.float32) + norm_back(ffn_back, normed_two, scale_two, gain_two)
    mixed_grad = middle_grad.astype(jnp.bfloat16)
    out_grad = dot_tn(attended, mixed_grad)
    attended_grad = dot_nt(mixed_grad, w_out).astype(jnp.bfloat16)

    cut, deep = query_proj.shape[0], down_proj.shape[0]
    plane = lambda a: lax.psum_scatter(a, ("x", "y"), scatter_dimension=0, tiled=True)
    down_sum = jnp.concatenate(core_sums([down_grad, out_grad], [deep, cut]), axis=1)
    pair = core_sums([gate_grad, up_grad], [cut] * 2)
    attended_grad, down_sum, pair = fence(attended_grad, whole(down_sum), pair)
    down_sum = plane(down_sum)
    pair = pair_first(*pair)

    dq, dk, dv, diag, dfar = attention_backward(
        queries, keys, values, attended_grad, attended, logs, q_label, k_label, base, far
    )
    up_z, down_z = bits("z"), bits("z")[::-1]
    near_z, rest_z = up_z[:1], up_z[1:]

    dq, dk, dv, diag, dfar, pair = fence(dq, dk, dv, diag, dfar, pair)
    pair = pair_second(*pair)
    far_back = dot_nt(dk[near_len:], w_key) + dot_nt(dv[near_len:], w_value)
    side_back = scatter_over(far_back.astype(jnp.bfloat16), "z", down_z[:-1])
    query_grad = dot_tn(normed, dq).astype(jnp.bfloat16)
    key_grad = dot_tn(key_rows, dk).astype(jnp.bfloat16)
    value_grad = dot_tn(key_rows, dv).astype(jnp.bfloat16)

    dq, dk, dv, query_grad, key_grad, value_grad, side_back, pair = fence(
        dq, dk, dv, query_grad, key_grad, value_grad, side_back, pair
    )
    three = jnp.concatenate(core_sums([query_grad, key_grad, value_grad], [cut] * 3), axis=1)
    pair = scatter_over(pair, "z", near_z)
    side_back = scatter_over(side_back, "z", down_z[-1:])
    key_back = dot_nt(dk[:near_len], w_key) + dot_nt(dv[:near_len], w_value)
    own_start = reach * rows
    normed_back = dot_nt(dq, w_query) + key_back[own_start : own_start + rows]
    back_low = key_back.astype(jnp.bfloat16)

    three, normed_back, back_low, side_back, pair, down_sum = fence(
        whole(three), normed_back, back_low, side_back, pair, down_sum
    )
    down_sum = scatter_over(down_sum, "z", near_z)
    three = scatter_over(three, "x", bits("x"))
    pair = scatter_over(pair, "z", rest_z)
    side_back = scatter_over(side_back, "y", [1]).astype(jnp.float32)
    low_y = lax.axis_index("y") == 0
    blocks = back_low.reshape(2 * reach + 1, rows, width)
    near_by = jnp.where(low_y, blocks[3], blocks[1])
    farther = jnp.where(low_y, blocks[1], blocks[3])
    got = swapped(jnp.stack([near_by, farther]), "y")

    three, got, side_back, normed_back, blocks, pair, down_sum = fence(
        three, got, side_back, normed_back, blocks, pair, down_sum
    )
    down_sum = scatter_over(down_sum, "z", rest_z)
    three = scatter_over(three, "y", [1])
    pair = gather_over(pair, "z", rest_z[::-1])
    zero = jnp.zeros_like(got[1])
    upward = shifted(add_low(blocks[4], jnp.where(low_y, got[1], zero)), "z", 1)
    downward = shifted(add_low(blocks[0], jnp.where(low_y, zero, got[1])), "z", -1)
    got = [got[0], upward, downward]
    global_part = jnp.sum(side_back * normed_side, axis=0)
    sums_grad = norm_back(side_back, normed_side, scale_side, gain_side)
    normed_back = (
        normed_back.reshape(own_blocks, GB, width) + sums_grad[:, None, :]
    ).reshape(rows, width)

    diag = diag.reshape(H, 8, table_width)
    near_sum = diag[:, 0]
    for r in range(1, 8):
        near_sum = near_sum + jnp.roll(diag[:, r], -r, axis=1)
    near_sum = near_sum[:, LANES + 1 : LANES + 2 * HALF]
    local_part = lax.dot_general(
        near_sum, onehot_near.astype(jnp.float32), (((1,), (0,)), ((), ())), precision=HIGHEST
    )
    dfar = dfar.reshape(H, own_blocks, far_len)
    side_sum = sum(
        jnp.pad(dfar[:, r], ((0, 0), (own_blocks - 1 - r, r))) for r in range(own_blocks)
    )
    side_part = lax.dot_general(
        side_sum, onehot_side.astype(jnp.float32), (((1,), (0,)), ((), ())), precision=HIGHEST
    )

    three, normed_back, got, local_part, side_part, global_part, pair, down_sum = fence(
        three, normed_back, got, local_part, side_part, global_part, pair, down_sum
    )
    three = scatter_over(three, "z", near_z)
    pair = gather_over(pair, "z", near_z)
    down_sum = gather_over(down_sum, "z", rest_z[::-1])
    for piece in got:
        normed_back = normed_back + piece.astype(jnp.float32)
    first_part = jnp.sum(normed_back * normed_one, axis=0)
    hidden_grad = (
        middle_grad + norm_back(normed_back, normed_one, scale_one, gain_one)
    ).astype(jnp.bfloat16)
    tables = jnp.concatenate([local_part, side_part], axis=0)
    tiny = jnp.concatenate(
        [
            jnp.stack([first_part, second_part, global_part]),
            jnp.pad(tables, ((0, 5), (0, width - tables.shape[1]))),
        ]
    )

    three = scatter_over(three, "z", rest_z)
    pair = gather_over(pair, "y", [1])
    down_sum = gather_over(down_sum, "z", near_z)
    tiny = tiny + swapped(tiny, "c")
    tiny = tiny + swapped(tiny, "x")

    three, tiny, pair, down_sum = fence(three, tiny, pair, down_sum)
    three = gather_over(three, "z", rest_z[::-1])
    down_sum = gather_over(down_sum, "y", [1])
    tiny = tiny + swapped(tiny, "y")

    three = gather_over(three, "z", near_z)
    for bit in near_z:
        tiny = tiny + swapped(tiny, "z", bit)

    three, tiny = fence(three, tiny)
    three = gather_over(three, "y", [1]).reshape(3, cut, -1)
    for bit in rest_z:
        tiny = tiny + swapped(tiny, "z", bit)
    pair = pair.reshape(2, 2, cut // 2, -1)
    pair = pair[:, 0].reshape(cut, -1), pair[:, 1].reshape(cut, -1)
    big = [three[0], three[1], three[2], down_sum[deep:], pair[0], pair[1], down_sum[:deep]]
    big = [a.astype(jnp.float32) for a in big]
    shards = lax.axis_size(SHARD)
    shard = lax.axis_index(SHARD)
    own = lax.dynamic_slice_in_dim(tiny[:3], shard * cut, cut, 1)
    bias_rows = NB // shards
    own_tables = lax.dynamic_slice_in_dim(tiny[3 : 3 + 2 * H, :NB], shard * bias_rows, bias_rows, 1).T
    done = [own[0], own[1], own[2], own_tables[:, :H], own_tables[:, H:]]
    return (outputs[None], hidden_grad[None], *big, *done)


def solution(mesh):
    ctx, shard = mesh.shape["ctx"], mesh.shape["shard"]
    fine = jax.sharding.Mesh(
        mesh.devices.reshape(ctx // 2, 2, shard // 2, 2), CTX + SHARD
    )
    tokens = P(SHARD, CTX, None)
    weight = P(SHARD, None)
    gain = P(SHARD)
    return jax.shard_map(
        on_device,
        mesh=fine,
        in_specs=(tokens, tokens) + (weight,) * 7 + (gain,) * 3 + (weight,) * 3 + (P(), P()),
        out_specs=(tokens, tokens) + (weight,) * 7 + (gain,) * 3 + (weight,) * 2,
        check_vma=False,
    )
```
